512 devices in a mesh: lead: 8 (over z_lo), gy: 4 (over y), gx: 16 (over x, z_hi, core).
Axes of the slice: x: 4, y: 4, z: 16 (z_hi: 2, z_lo: 8; z = z_hi * 8 + z_lo), core: 2. Of those that a mesh axis runs over, the one named last changes fastest.
Arguments:
- inputs: bfloat16 [8, 256, 128, 256], P('lead', 'gy', 'gx'), may hold values from -6 to 6
- lead_ids: int32 [8], P('lead'), may hold values from 0 to 359
- film: float32 [360, 4, 256], replicated, may hold values from -3 to 3
- flat_weights: bfloat16 [2, 589824], P(None, ('lead', 'gy', 'gx')), may hold values from -0.25 to 0.25
- cotangent: bfloat16 [8, 256, 128, 256], P('lead', 'gy', 'gx'), may hold values from -6 to 6
Outputs:
- outputs: bfloat16 [8, 256, 128, 256], P('lead', 'gy', 'gx')
- weight_grad: float32 [589824], P(('lead', 'gy', 'gx'))
The draws below stay inside these ranges and needn't reach their ends.
All inputs are finite; a program needn't handle non-finite values.
Results may differ from the reference program's by a relative error of at most 0.0047.
Values may be sent and summed in bfloat16 or wider, within the bound.
A program may use at most 64 MiB of HBM per device.

```python
import math
import jax
import jax.numpy as jnp
from jax import lax

CHANNEL_COUNT = 256
LEAD_TIMES = 360
TILE_R = 64
TILE_C = 8
FIRST_DILATION = 64
SECOND_DILATION = 128
LEADS = 8
GRID_ROWS = 256
GRID_COLUMNS = 128
FLAT = 589824
N_GY = 4
N_GX = 16


def set_ends(drawn, stream_key, smallest, largest):
    shape = drawn.shape
    index_at = [jax.random.randint(jax.random.fold_in(stream_key, axis), (), 0, shape[axis]) for axis in range(len(shape))]
    drawn = drawn.at[tuple(index_at)].set(smallest)
    longest = shape.index(max(shape))
    index_at[longest] = (index_at[longest] + 1) % shape[longest]
    return drawn.at[tuple(index_at)].set(largest)


def shard_levels(own_key, shape, cuts, smallest, high):
    factor_of, own = 1.0, jax.random.fold_in(own_key, 6)
    for dim, blocks in cuts:
        heights = jnp.exp(jax.random.uniform(jax.random.fold_in(own, dim), (blocks,), jnp.float32, smallest / len(cuts), high / len(cuts)))
        factor_of = factor_of * jnp.repeat(heights, shape[dim] // blocks).reshape([-1 if axis == dim else 1 for axis in range(len(shape))])
    return factor_of


def bell_draw(stream_key, shape, deviation, limit, cuts=(), dtype=jnp.bfloat16):
    loudness = shard_levels(stream_key, shape, cuts, -0.22, 0.18) if cuts else 1.0
    drawn = jax.random.normal(stream_key, shape, jnp.float32) * deviation * loudness
    return jnp.minimum(jnp.maximum(drawn, -limit), limit).astype(dtype)


def setup_inputs(seed: int = 0) -> dict:
    key_of = jax.random.split(jax.random.key(seed), 6)
    inputs = bell_draw(key_of[0], (LEADS, GRID_ROWS, GRID_COLUMNS, CHANNEL_COUNT), 1.0, 6.0, ((0, 8), (1, 4), (2, 16)))
    lead_ids = set_ends(jax.random.randint(key_of[1], (LEADS,), 0, LEAD_TIMES), jax.random.fold_in(key_of[1], 1), 0, LEAD_TIMES - 1).astype(jnp.int32)
    film = bell_draw(key_of[2], (LEAD_TIMES, 4, CHANNEL_COUNT), 0.5, 3.0, (), jnp.float32)
    flat_weights = bell_draw(key_of[3], (2, FLAT), (9 * CHANNEL_COUNT // 4) ** -0.5, 0.25, ((1, 512),))
    cotangent = bell_draw(key_of[4], (LEADS, GRID_ROWS, GRID_COLUMNS, CHANNEL_COUNT), 1.0, 6.0, ((0, 8), (1, 4), (2, 16)))
    return dict(inputs=inputs, lead_ids=lead_ids, film=film, flat_weights=flat_weights, cotangent=cotangent)


def shifted(weather_field, row_off, col_off, dilation):
    padded = jnp.pad(weather_field, ((dilation, dilation), (dilation, dilation), (0, 0)))
    top = dilation + row_off * dilation
    left = dilation + col_off * dilation
    return padded[top:top + GRID_ROWS, left:left + GRID_COLUMNS]

def unfold_patches(weather_field, dilation, sign):
    pieces = []
    for row_off in (-1, 0, 1):
        for col_off in (-1, 0, 1):
            pieces.append(shifted(weather_field, sign * row_off, sign * col_off, dilation))
    return jnp.concatenate(pieces, axis=-1).reshape(GRID_ROWS * GRID_COLUMNS, 9 * CHANNEL_COUNT)

def reference(inputs, lead_ids, film, flat_weights, cotangent):
    highest = lax.Precision.HIGHEST
    weights = flat_weights.astype(jnp.float32).reshape(2, 3, 3, CHANNEL_COUNT, CHANNEL_COUNT)
    matrix_a = weights[0].reshape(9 * CHANNEL_COUNT, CHANNEL_COUNT)
    matrix_b = weights[1].reshape(9 * CHANNEL_COUNT, CHANNEL_COUNT)
    matrix_t = jnp.transpose(weights[1], (0, 1, 3, 2)).reshape(9 * CHANNEL_COUNT, CHANNEL_COUNT)
    scale = 1.0 / math.sqrt(LEADS * GRID_ROWS * GRID_COLUMNS)

    def one_lead(total, items):
        weather_field, lead, upstream_raw = items
        film_row = lax.dynamic_index_in_dim(film, lead, 0, keepdims=False)
        mult_a = 1.0 + film_row[0]
        shift_a = film_row[1]
        mult_b = 1.0 + film_row[2]
        shift_b = film_row[3]
        input_columns = unfold_patches(weather_field, FIRST_DILATION, 1).astype(jnp.float32)
        pre_a = jnp.dot(input_columns, matrix_a, precision=highest) * mult_a + shift_a
        sig_a = jax.nn.sigmoid(pre_a)
        hidden_state = (weather_field.reshape(-1, CHANNEL_COUNT).astype(jnp.float32) + pre_a * sig_a).astype(jnp.bfloat16)
        hidden_columns = unfold_patches(hidden_state.reshape(GRID_ROWS, GRID_COLUMNS, CHANNEL_COUNT), SECOND_DILATION, 1).astype(jnp.float32)
        pre_b = jnp.dot(hidden_columns, matrix_b, precision=highest) * mult_b + shift_b
        sig_b = jax.nn.sigmoid(pre_b)
        result = (hidden_state.astype(jnp.float32) + pre_b * sig_b).astype(jnp.bfloat16)
        upstream = upstream_raw.reshape(-1, CHANNEL_COUNT).astype(jnp.float32)
        second_gradient = (upstream * mult_b * sig_b * (1.0 + pre_b * (1.0 - sig_b))).astype(jnp.bfloat16)
        column_gradient = unfold_patches(second_gradient.reshape(GRID_ROWS, GRID_COLUMNS, CHANNEL_COUNT), SECOND_DILATION, -1).astype(jnp.float32)
        back = upstream + jnp.dot(column_gradient, matrix_t, precision=highest)
        grad_a = (back * mult_a * sig_a * (1.0 + pre_a * (1.0 - sig_a))).astype(jnp.bfloat16)
        blocks_in = input_columns.reshape(N_GY, TILE_R, N_GX, TILE_C, 9 * CHANNEL_COUNT)
        blocks_grad = grad_a.astype(jnp.float32).reshape(N_GY, TILE_R, N_GX, TILE_C, CHANNEL_COUNT)

        def per_row(pair):
            left_part, right_part = pair
            return jnp.einsum('rxck,rxco->ko', left_part, right_part, precision=highest) * scale
        parts = lax.map(per_row, (blocks_in, blocks_grad))
        return (total + lax.optimization_barrier(jnp.sum(parts, axis=0)), result.reshape(GRID_ROWS, GRID_COLUMNS, CHANNEL_COUNT))
    total, results = lax.scan(one_lead, jnp.zeros((9 * CHANNEL_COUNT, CHANNEL_COUNT), jnp.float32), (inputs, lead_ids, cotangent))
    return (results, total.reshape(-1))
```

```python
import functools
import math

import jax
import jax.numpy as jnp
from jax import lax
from jax.experimental import pallas as pl
from jax.experimental.pallas import tpu as pltpu
from jax.sharding import PartitionSpec as P

FIRST_DILATION = 64
SECOND_DILATION = 128
MESH = pl.DeviceIdType.MESH
DMA = pltpu.SemaphoreType.DMA
F32, BF16 = jnp.float32, jnp.bfloat16


def place():
    lead, gy, gx = lax.axis_index("lead"), lax.axis_index("gy"), lax.axis_index("gx")
    return lead, gy, gx, gx // 4, (gx // 2) % 2, gx % 2


def remote(src, dst, send_sem, recv_sem, **where):
    return pltpu.make_async_remote_copy(
        src_ref=src, dst_ref=dst, send_sem=send_sem, recv_sem=recv_sem, device_id=where, device_id_type=MESH
    )


def greet():
    lead, gy, gx, x, zh, core = place()
    barrier = pltpu.get_barrier_semaphore()

    @pl.loop(1, 16)
    def _(k):
        pl.semaphore_signal(barrier, inc=1, device_id={"gx": (gx + k) % 16}, device_id_type=MESH)

    @pl.loop(1, 16)
    def _(k):
        z = (zh * 8 + lead + k) % 16
        pl.semaphore_signal(
            barrier, inc=1, device_id={"lead": z % 8, "gx": x * 4 + (z // 8) * 2 + core}, device_id_type=MESH
        )

    for k in range(1, 4):
        pl.semaphore_signal(barrier, inc=1, device_id={"gy": (gy + k) % 4}, device_id_type=MESH)
    pl.semaphore_wait(barrier, 33)


def gather_kernel(w_ref, W, G, s1, r1, s2, r2, s3, r3, s4, r4, s5, r5):
    lead, gy, gx, x, zh, core = place()
    greet()
    builder = gx // 2 == (lead // 2) * 2 + lead % 2

    def to_builder(c):
        return remote(
            w_ref, G.at[gx], s1.at[c], r1.at[gx], gx=(lead // 2) * 4 + (lead % 2) * 2 + c
        )

    def is_other(c):
        return gx != (lead // 2) * 4 + (lead % 2) * 2 + c

    for c in range(2):

        @pl.when(is_other(c))
        def _():
            to_builder(c).start()

    def spread(k):
        z = (zh * 8 + lead + k) % 16
        piece = W.at[core, :, lead, gy]
        return remote(piece, piece, s2.at[k], r2.at[lead % 2], lead=z % 8, gx=x * 4 + (z // 8) * 2 + core)

    @pl.when(builder)
    def _():
        G[gx] = w_ref[...]

        @pl.loop(1, 16)
        def _(k):
            remote(w_ref, G.at[(gx + k) % 16], s1.at[0], r1.at[(gx + k) % 16], gx=gx).wait_recv()

        flat = G[...].reshape(512, 128)
        row = lax.broadcasted_iota(jnp.int32, (72, 512), 0) * 2 + core
        col = lax.broadcasted_iota(jnp.int32, (72, 512), 1)
        owner = (row * 57) >> 9
        want = owner * 32 + (row - owner * 9)
        for block in range(2):
            pick = (col == want + block * 16).astype(F32).astype(BF16)
            W[core, block, lead, gy] = jnp.dot(pick, flat, preferred_element_type=F32).astype(BF16)

        @pl.loop(1, 16)
        def _(k):
            spread(k).start()

    for j in range(2):
        own = jnp.logical_and(lead == 2 * x + j, zh == j)

        @pl.when(jnp.logical_not(own))
        def _():
            piece = W.at[core, :, 2 * x + j, gy]
            remote(piece, piece, s2.at[0], r2.at[j], gx=gx).wait_recv()

    def over_y(k, start):
        piece = W.at[core, :, pl.ds(2 * x, 2), gy if start else (gy + 4 - k) % 4]
        return remote(piece, piece, s3.at[k - 1], r3.at[k - 1], gy=(gy + k) % 4)

    for k in (1, 3, 2):
        over_y(k, True).start()
    for k in (1, 3, 2):
        over_y(k, False).wait_recv()

    def over_x(k, start):
        piece = W.at[core, :, pl.ds(2 * (x if start else (x + 4 - k) % 4), 2)]
        return remote(piece, piece, s4.at[k - 1], r4.at[k - 1], gx=((x + k) % 4) * 4 + gx % 4)

    def to_mate(k, start):
        piece = W.at[core if start else 1 - core, :, pl.ds(2 * ((x + 4 - k) % 4), 2)]
        return remote(piece, piece, s5.at[k], r5.at[k], gx=gx + 1 - 2 * core)

    for k in (1, 3, 2):
        over_x(k, True).start()
    to_mate(0, True).start()
    for k in (1, 3, 2):
        over_x(k, False).wait_recv()
        to_mate(k, True).start()
    for k in (0, 1, 3, 2):
        to_mate(k, False).wait_recv()

    for c in range(2):

        @pl.when(is_other(c))
        def _():
            to_builder(c).wait_send()

    @pl.when(builder)
    def _():
        @pl.loop(1, 16)
        def _(k):
            spread(k).wait_send()

    for k in range(1, 4):
        over_y(k, True).wait_send()
        over_x(k, True).wait_send()
    for k in range(4):
        to_mate(k, True).wait_send()


def gather_weights(flat_weights):
    padded = jnp.pad(flat_weights.reshape(2, 9, 128), ((0, 0), (0, 7), (0, 0)))
    return pl.pallas_call(
        gather_kernel,
        out_shape=jax.ShapeDtypeStruct((2, 2, 8, 4, 72, 128), BF16),
        in_specs=[pl.BlockSpec(memory_space=pltpu.VMEM)],
        out_specs=pl.BlockSpec(memory_space=pltpu.VMEM),
        scratch_shapes=[
            pltpu.VMEM((16, 2, 16, 128), BF16),
            DMA((2,)), DMA((16,)),
            DMA((16,)), DMA((2,)),
            DMA((3,)), DMA((3,)),
            DMA((3,)), DMA((3,)),
            DMA((4,)), DMA((4,)),
        ],
        compiler_params=pltpu.CompilerParams(
            collective_id=0, has_side_effects=True, vmem_limit_bytes=40 << 20
        ),
    )(padded)


def scatter_kernel(term, out, RC, T, RX, A1, RY, A2, RZ, F, S, RF, s1, r1, s2, r2, s3, r3, s4, r4, s5, r5):
    lead, gy, gx, x, zh, core = place()
    greet()
    zid = zh * 8 + lead
    mate = remote(term.at[1 - core], RC, s1, r1, gx=gx + 1 - 2 * core)
    mate.start()
    mate.wait_recv()

    @pl.loop(0, 8)
    def _(i):
        T[i] = (term[core, i] + RC[i]).astype(BF16)

    def over_x(k):
        return remote(
            T.at[pl.ds(2 * ((x + k) % 4), 2)], RX.at[k - 1], s2.at[k - 1], r2.at[k - 1], gx=((x + k) % 4) * 4 + gx % 4
        )

    for k in (1, 3, 2):
        over_x(k).start()
    for k in (1, 3, 2):
        over_x(k).wait_recv()
    for j in range(2):
        A1[j] = (
            term[core, 2 * x + j]
            + RC[2 * x + j]
            + RX[0, j].astype(F32)
            + RX[1, j].astype(F32)
            + RX[2, j].astype(F32)
        )

    def over_y(k):
        return remote(A1.at[:, (gy + k) % 4], RY.at[k - 1], s3.at[k - 1], r3.at[k - 1], gy=(gy + k) % 4)

    for k in (1, 3, 2):
        over_y(k).start()
    for k in (1, 3, 2):
        over_y(k).wait_recv()
    for j in range(2):
        A2[j] = A1[j, gy] + RY[0, j] + RY[1, j] + RY[2, j]

    def over_z(j):
        return remote(A2.at[j], RZ.at[zid], s4.at[j], r4.at[zid], lead=2 * x + j, gx=x * 4 + j * 2 + core)

    def other(j):
        return jnp.logical_or(lead != 2 * x + j, zh != j)

    for j in range(2):

        @pl.when(other(j))
        def _():
            over_z(j).start()

    def piece(k):
        return remote(S.at[(gx + k) % 16], RF.at[core], s5.at[k], r5.at[core], gx=(gx + k) % 16)

    builder = gx // 2 == (lead // 2) * 2 + lead % 2

    @pl.when(builder)
    def _():
        F[pl.ds(0, 72), :] = A2[lead % 2]
        F[pl.ds(72, 8), :] = jnp.zeros((8, 128), F32)

        @pl.loop(1, 16)
        def _(k):
            src = (zid + k) % 16
            remote(A2.at[0], RZ.at[src], s4.at[0], r4.at[src], gx=gx).wait_recv()
            F[pl.ds(0, 72), :] += RZ[src]

        for half in range(2):

            @pl.when(core == half)
            def _():
                for to in range(16):
                    first = (9 * to - half + 1) // 2
                    S[to] = F[first : first + 8, :]

        RF[core] = S[gx]

        @pl.loop(1, 16)
        def _(k):
            piece(k).start()

    for c in range(2):

        @pl.when(jnp.logical_or(jnp.logical_not(builder), core != c))
        def _():
            remote(S.at[0], RF.at[c], s5.at[0], r5.at[c], gx=gx).wait_recv()

    even, odd = RF[core], RF[1 - core]
    for j in range(9):
        out[j : j + 1, :] = (odd if j % 2 else even)[j // 2 : j // 2 + 1, :]

    mate.wait_send()
    for k in range(1, 4):
        over_x(k).wait_send()
        over_y(k).wait_send()
    for j in range(2):

        @pl.when(other(j))
        def _():
            over_z(j).wait_send()

    @pl.when(builder)
    def _():
        @pl.loop(1, 16)
        def _(k):
            piece(k).wait_send()


def scatter_sum(term):
    return pl.pallas_call(
        scatter_kernel,
        out_shape=jax.ShapeDtypeStruct((9, 128), F32),
        in_specs=[pl.BlockSpec(memory_space=pltpu.VMEM)],
        out_specs=pl.BlockSpec(memory_space=pltpu.VMEM),
        scratch_shapes=[
            pltpu.VMEM((8, 4, 72, 128), F32),
            pltpu.VMEM((8, 4, 72, 128), BF16),
            pltpu.VMEM((3, 2, 4, 72, 128), BF16),
            pltpu.VMEM((2, 4, 72, 128), F32),
            pltpu.VMEM((3, 2, 72, 128), F32),
            pltpu.VMEM((2, 72, 128), F32),
            pltpu.VMEM((16, 72, 128), F32),
            pltpu.VMEM((80, 128), F32),
            pltpu.VMEM((16, 8, 128), F32),
            pltpu.VMEM((2, 8, 128), F32),
            DMA(()), DMA(()),
            DMA((3,)), DMA((3,)),
            DMA((3,)), DMA((3,)),
            DMA((2,)), DMA((16,)),
            DMA((16,)), DMA((2,)),
        ],
        compiler_params=pltpu.CompilerParams(
            collective_id=1, has_side_effects=True, vmem_limit_bytes=40 << 20
        ),
    )(term)


def passed_along(value, axis, steps):
    count = lax.axis_size(axis)
    leading, last = (max(0, -steps), min(count, count - steps))
    return lax.ppermute(value, axis, [(source, source + steps) for source in range(leading, last)])


def adjacent_cells(weather_field, row_step, col_step):
    row_list = [-1, 0, 1]
    col_list = [-1, 0, 1] if col_step < lax.axis_size("gx") else [0]
    taps = []
    stacked = jnp.stack(
        [
            (
                weather_field
                if row_off == 0
                else passed_along(weather_field, "gy", -row_off * row_step)
            )
            for row_off in row_list
        ]
    )
    columns = [
        stacked if col_off == 0 else passed_along(stacked, "gx", -col_off * col_step)
        for col_off in col_list
    ]
    for col_off in col_list:
        for row_off in row_list:
            taps.append(
                (row_off, col_off, columns[col_list.index(col_off)][row_list.index(row_off)])
            )
    return taps


def lower(taps, weight_four, flipped):
    patch_width = weight_four.shape[-1]
    cols = jnp.concatenate(
        [piece.reshape(-1, patch_width) for row_off, col_off, piece in taps], axis=1
    )
    blocks = []
    for row_off, col_off, piece in taps:
        if flipped:
            blocks.append(weight_four[1 - row_off, 1 - col_off].T)
        else:
            blocks.append(weight_four[row_off + 1, col_off + 1])
    return (cols, jnp.concatenate(blocks, axis=0))


def shards(inputs, lead_ids, film, flat_weights, cotangent):
    tile_row_count, tile_column_count, patch_width = (
        inputs.shape[1],
        inputs.shape[2],
        inputs.shape[3],
    )
    halves = gather_weights(flat_weights).reshape(2, 2, 2304, 128)
    gathered = jnp.concatenate([halves[0], halves[1]], axis=2)
    weight_a = gathered[0].reshape(3, 3, patch_width, patch_width)
    weight_b = gathered[1].reshape(3, 3, patch_width, patch_width)
    table_rows = film.shape[0]
    picker = (jnp.arange(table_rows, dtype=jnp.int32) == lead_ids[0]).astype(jnp.float32)
    film_row = jnp.dot(
        picker, film.reshape(table_rows, -1), precision=lax.Precision.HIGHEST
    ).reshape(4, patch_width)
    mult_a = 1.0 + film_row[0]
    shift_a = film_row[1]
    mult_b = 1.0 + film_row[2]
    shift_b = film_row[3]
    weather_field = inputs[0]
    input_kernel_taps = adjacent_cells(
        weather_field, FIRST_DILATION // tile_row_count, FIRST_DILATION // tile_column_count
    )
    input_columns, matrix_a = lower(input_kernel_taps, weight_a, False)
    pre_a = jnp.dot(input_columns, matrix_a, preferred_element_type=jnp.float32) * mult_a + shift_a
    sig_a = jax.nn.sigmoid(pre_a)
    hidden_state = (
        weather_field.reshape(-1, patch_width).astype(jnp.float32) + pre_a * sig_a
    ).astype(jnp.bfloat16)
    taps_hidden = adjacent_cells(
        hidden_state.reshape(tile_row_count, tile_column_count, patch_width),
        SECOND_DILATION // tile_row_count,
        SECOND_DILATION // tile_column_count,
    )
    hidden_columns, matrix_b = lower(taps_hidden, weight_b, False)
    pre_b = jnp.dot(hidden_columns, matrix_b, preferred_element_type=jnp.float32) * mult_b + shift_b
    sig_b = jax.nn.sigmoid(pre_b)
    outputs = (hidden_state.astype(jnp.float32) + pre_b * sig_b).astype(jnp.bfloat16)
    upstream = cotangent[0].reshape(-1, patch_width).astype(jnp.float32)
    second_gradient = (upstream * mult_b * sig_b * (1.0 + pre_b * (1.0 - sig_b))).astype(
        jnp.bfloat16
    )
    taps_grad = adjacent_cells(
        second_gradient.reshape(tile_row_count, tile_column_count, patch_width),
        SECOND_DILATION // tile_row_count,
        SECOND_DILATION // tile_column_count,
    )
    column_gradient, matrix_t = lower(taps_grad, weight_b, True)
    back = upstream + jnp.dot(column_gradient, matrix_t, preferred_element_type=jnp.float32)
    grad_a = (back * mult_a * sig_a * (1.0 + pre_a * (1.0 - sig_a))).astype(jnp.bfloat16)
    scale = 1.0 / math.sqrt(
        lax.axis_size(("lead", "gy", "gx")) * tile_row_count * tile_column_count
    )
    products = (
        lax.dot_general(
            input_columns, grad_a, (((0,), (0,)), ((), ())), preferred_element_type=jnp.float32
        )
        * scale
    )
    term = jnp.zeros((3, 3, patch_width, patch_width), jnp.float32)
    for number, (row_off, col_off, piece) in enumerate(input_kernel_taps):
        term = term.at[row_off + 1, col_off + 1].set(
            products[number * patch_width : (number + 1) * patch_width]
        )
    term = term.reshape(2304, 256)
    halves = jnp.stack([term[:, :128], term[:, 128:]]).reshape(2, 8, 4, 72, 128)
    total = scatter_sum(halves)
    return (outputs.reshape(inputs.shape), total.reshape(-1))


def solution(mesh):
    return jax.shard_map(
        shards,
        mesh=mesh,
        in_specs=(
            P("lead", "gy", "gx", None),
            P("lead"),
            P(),
            P(None, ("lead", "gy", "gx")),
            P("lead", "gy", "gx", None),
        ),
        out_specs=(P("lead", "gy", "gx", None), P(("lead", "gy", "gx"))),
        check_vma=False,
    )
```

```python
import jax
import jax.numpy as jnp
from jax import lax
from jax.experimental import pallas as pl
from jax.experimental.pallas import tpu as pltpu
from jax.sharding import PartitionSpec as P

MESH = pl.DeviceIdType.MESH
DMA = pltpu.SemaphoreType.DMA
F32, BF16 = jnp.float32, jnp.bfloat16


def place():
    lead, gy, gx = lax.axis_index("lead"), lax.axis_index("gy"), lax.axis_index("gx")
    return lead, gy, gx, gx // 4, (gx // 2) % 2, gx % 2


def remote(src, dst, send_sem, recv_sem, **where):
    return pltpu.make_async_remote_copy(
        src_ref=src, dst_ref=dst, send_sem=send_sem, recv_sem=recv_sem, device_id=where, device_id_type=MESH
    )


def greet():
    lead, gy, gx, x, zh, core = place()
    barrier = pltpu.get_barrier_semaphore()

    @pl.loop(1, 16)
    def _(k):
        pl.semaphore_signal(barrier, inc=1, device_id={"gx": (gx + k) % 16}, device_id_type=MESH)

    @pl.loop(1, 16)
    def _(k):
        z = (zh * 8 + lead + k) % 16
        pl.semaphore_signal(
            barrier, inc=1, device_id={"lead": z % 8, "gx": x * 4 + (z // 8) * 2 + core}, device_id_type=MESH
        )

    for k in range(1, 4):
        pl.semaphore_signal(barrier, inc=1, device_id={"gy": (gy + k) % 4}, device_id_type=MESH)
    @pl.when(gx // 2 == (lead // 2) * 2 + lead % 2)
    def _():
        @pl.loop(0, 16)
        def _(k):
            pl.semaphore_signal(
                barrier, inc=1, device_id={"gy": gy + 1 - 2 * (gy % 2), "gx": k}, device_id_type=MESH
            )

    pl.semaphore_wait(barrier, 35)


ROWS = 128
CHUNKS = 4


def group(lead, gy):
    return pl.ds(pl.multiple_of((lead * 2 + gy // 2) * 144, 16), 144)


def quarter(x):
    return pl.ds(pl.multiple_of(x * 576, 64), 576)


def sigmoid(v):
    return 1.0 / (1.0 + jnp.exp(-v))


def step_kernel(
    ids, w_ref, x_ref, film, cot, out, grad,
    W, G, X, XT, H, GB, GA, DA, ACC, TA, TB, RC, T, RX, A1, RY, A2, RZ, F, S, RF,
    hs, hr, cs, cr, es, er, s1, r1, s2, r2, s3, r3, s4, r4, s5, r5, m1, q1, m2, q2, m3, q3, m4, q4, m5, q5,
):
    lead, gy, gx, x, zh, core = place()
    zid = zh * 8 + lead
    builder = gx // 2 == (lead // 2) * 2 + lead % 2
    west = x // 2
    greet()

    def halo(col, up):
        src = x_ref if col == 0 else X.at[1, 1]
        return remote(
            src, X.at[col, 0 if up else 2], hs.at[col, int(up)], hr.at[col, int(up)],
            gy=(gy + (1 if up else 3)) % 4,
        )

    def halo_in(col, up):
        return remote(
            x_ref, X.at[col, 0 if up else 2], hs.at[col, int(up)], hr.at[col, int(up)], gy=(gy + (3 if up else 1)) % 4
        )

    across = remote(x_ref, X.at[1, 1], hs.at[2, 0], hr.at[2, 0], gx=(gx + 8) % 16)
    has = {True: gy < 3, False: gy > 0}
    gets = {True: gy > 0, False: gy < 3}

    block = gy % 2
    built = (lead // 2) * 4 + (lead % 2) * 2

    def to_builder(c, y):
        return remote(
            w_ref.at[y], G.at[block, gx], s1.at[c, y], r1.at[block, gx], gy=gy - block + y, gx=built + c
        )

    def is_other(c, y):
        return jnp.logical_or(gx != built + c, block != y)

    for c in range(2):
        for y in range(2):

            @pl.when(is_other(c, y))
            def _():
                to_builder(c, y).start()

    across.start()
    for up in (True, False):

        @pl.when(has[up])
        def _():
            halo(0, up).start()

        @pl.when(jnp.logical_not(gets[up]))
        def _():
            for col in range(2):
                X[col, 0 if up else 2] = jnp.zeros((512, 256), BF16)

    def spread(k):
        z = (zid + k) % 16
        piece = W.at[core, block, group(lead, gy)]
        return remote(piece, piece, s2.at[k], r2.at[lead % 2], lead=z % 8, gx=x * 4 + (z // 8) * 2 + core)

    @pl.when(builder)
    def _():
        G[block, gx] = w_ref[block]

        @pl.loop(1, 32)
        def _(k):
            src = (block * 16 + gx + k) % 32
            remote(w_ref.at[0], G.at[src // 16, src % 16], s1.at[0, 0], r1.at[src // 16, src % 16], gx=gx).wait_recv()

        flat = G[...].reshape(512, 128)
        row = lax.broadcasted_iota(jnp.int32, (144, 512), 0) * 2 + core
        col = lax.broadcasted_iota(jnp.int32, (144, 512), 1)
        owner = (row * 57) >> 9
        pick = (col == owner * 16 + (row - owner * 9)).astype(F32).astype(BF16)
        W[core, block, group(lead, gy), :] = jnp.dot(pick, flat, preferred_element_type=F32).astype(BF16)

        @pl.loop(1, 16)
        def _(k):
            spread(k).start()

    across.wait_recv()
    for up in (True, False):

        @pl.when(has[up])
        def _():
            halo(1, up).start()

    X[0, 1] = x_ref[...]
    XT[0, 1] = x_ref[...].T
    XT[1, 1] = X[1, 1].T
    for col in range(2):
        for up in (True, False):

            @pl.when(gets[up])
            def _():
                halo_in(col, up).wait_recv()

            XT[col, 0 if up else 2] = X[col, 0 if up else 2].T

    for j in range(2):
        own = jnp.logical_and(lead == 2 * x + j, zh == j)

        @pl.when(jnp.logical_not(own))
        def _():
            piece = W.at[core, block, group(2 * x + j, gy)]
            remote(piece, piece, s2.at[0], r2.at[j], gx=gx).wait_recv()

    def over_y(k, j, start):
        y = gy if start else (gy + 4 - k) % 4
        piece = W.at[core, y % 2, group(2 * x + j, y)]
        return remote(piece, piece, s3.at[k - 1, j], r3.at[k - 1, j], gy=(gy + k) % 4)

    for j in range(2):
        for k in (1, 3, 2):
            over_y(k, j, True).start()
    for j in range(2):
        for k in (1, 3, 2):
            over_y(k, j, False).wait_recv()

    def over_x(k, start):
        piece = W.at[core, :, quarter(x if start else (x + 4 - k) % 4)]
        return remote(piece, piece, s4.at[k - 1], r4.at[k - 1], gx=((x + k) % 4) * 4 + gx % 4)

    def to_mate(k, start):
        piece = W.at[core if start else 1 - core, :, quarter((x + 4 - k) % 4)]
        return remote(piece, piece, s5.at[k], r5.at[k], gx=gx + 1 - 2 * core)

    for k in (1, 3, 2):
        over_x(k, True).start()
    to_mate(0, True).start()
    for k in (1, 3, 2):
        over_x(k, False).wait_recv()
        to_mate(k, True).start()
    for k in (0, 1, 3, 2):
        to_mate(k, False).wait_recv()

    row = film[ids[0]]
    mult_a, shift_a, mult_b, shift_b = 1.0 + row[0:1], row[1:2], 1.0 + row[2:3], row[3:4]

    def half(h, block, tap):
        return W[h, block, pl.ds(pl.multiple_of(tap * 256, 256), 256), :]

    def weight(block, tap):
        return jnp.concatenate([half(0, block, tap), half(1, block, tap)], axis=1)

    taps = [(0, 1, 1 + 3), (0, 0, 1), (0, 2, 7)] + [(1, a, 3 * a + 2 - 2 * west) for a in (1, 0, 2)]

    def rows_of(m):
        return pl.ds(pl.multiple_of(m * ROWS, ROWS), ROWS)

    def send_hidden(m):
        return remote(H.at[0, rows_of(m)], H.at[1, rows_of(m)], cs.at[m], cr.at[m], gy=(gy + 2) % 4)

    @pl.loop(0, CHUNKS)
    def _(m):
        r = rows_of(m)
        pre = jnp.zeros((ROWS, 256), F32)
        for col, a, tap in taps:
            pre = pre + jnp.dot(X[col, a, r, :], weight(0, tap), preferred_element_type=F32)
        pre = pre * mult_a + shift_a
        sig = sigmoid(pre)
        H[0, r, :] = (x_ref[r, :].astype(F32) + pre * sig).astype(BF16)
        DA[r, :] = mult_a * sig * (1.0 + pre * (1.0 - sig))
        send_hidden(m).start()

    south = gy // 2

    @pl.loop(0, CHUNKS)
    def _(m):
        r = rows_of(m)
        ACC[r, :] = jnp.dot(H[0, r, :], weight(1, 4), preferred_element_type=F32)

    def send_grad(m):
        return remote(GB.at[0, rows_of(m)], GB.at[1, rows_of(m)], es.at[m], er.at[m], gy=(gy + 2) % 4)

    @pl.loop(0, CHUNKS)
    def _(m):
        r = rows_of(m)
        send_hidden(m).wait_recv()
        pre = ACC[r, :] + jnp.dot(H[1, r, :], weight(1, 7 - 6 * south), preferred_element_type=F32)
        pre = pre * mult_b + shift_b
        sig = sigmoid(pre)
        up = cot[r, :].astype(F32)
        GB[0, r, :] = (up * mult_b * sig * (1.0 + pre * (1.0 - sig))).astype(BF16)
        send_grad(m).start()
        out[r, :] = (H[0, r, :].astype(F32) + pre * sig).astype(BF16)

    def back_dot(value, tap):
        turned = (((1,), (1,)), ((), ()))
        return lax.dot_general(
            value[:, :128], half(0, 1, tap), turned, preferred_element_type=F32
        ) + lax.dot_general(value[:, 128:], half(1, 1, tap), turned, preferred_element_type=F32)

    @pl.loop(0, CHUNKS)
    def _(m):
        r = rows_of(m)
        ACC[r, :] = cot[r, :].astype(F32) + back_dot(GB[0, r, :], 4)

    @pl.loop(0, CHUNKS)
    def _(m):
        r = rows_of(m)
        send_grad(m).wait_recv()
        back = ACC[r, :] + back_dot(GB[1, r, :], 1 + 6 * south)
        value = back * DA[r, :]
        left, right = value[:, :128], value[:, 128:]
        GA[r, :] = jnp.concatenate(
            [jnp.where(core == 0, left, right), jnp.where(core == 0, right, left)], axis=1
        ).astype(BF16)

    scale = 1.0 / 512.0

    def mate(tap):
        return remote(TB.at[tap], RC.at[tap], m1.at[tap], q1.at[tap], gx=gx + 1 - 2 * core)

    for col, a, tap in taps:
        term = jnp.dot(XT[col, a], GA[...], preferred_element_type=F32) * scale
        TB[tap] = term[:, 128:]
        mate(tap).start()
        TA[pl.ds(pl.multiple_of(tap * 256, 256), 256), :] = term[:, :128]
    for a in range(3):
        at = pl.ds(pl.multiple_of((3 * a + 2 * west) * 256, 256), 256)
        TA[at, :] = jnp.zeros((256, 128), F32)
        T[at, :] = jnp.zeros((256, 128), BF16)
    for col, a, tap in taps:
        at = pl.ds(pl.multiple_of(tap * 256, 256), 256)
        mate(tap).wait_recv()
        both = TA[at, :] + RC[tap]
        TA[at, :] = both
        T[at, :] = both.astype(BF16)

    def sum_x(k):
        return remote(
            T.at[quarter((x + k) % 4)], RX.at[k - 1], m2.at[k - 1], q2.at[k - 1], gx=((x + k) % 4) * 4 + gx % 4
        )

    for k in (1, 3, 2):
        sum_x(k).start()
    for k in (1, 3, 2):
        sum_x(k).wait_recv()
    mine = TA[quarter(x), :] + RX[0].astype(F32) + RX[1].astype(F32) + RX[2].astype(F32)
    A1[...] = mine.reshape(2, 4, 72, 128)

    def sum_y(k):
        return remote(A1.at[:, (gy + k) % 4], RY.at[k - 1], m3.at[k - 1], q3.at[k - 1], gy=(gy + k) % 4)

    for k in (1, 3, 2):
        sum_y(k).start()
    for k in (1, 3, 2):
        sum_y(k).wait_recv()
    for j in range(2):
        A2[j] = A1[j, gy] + RY[0, j] + RY[1, j] + RY[2, j]

    def sum_z(j):
        return remote(A2.at[j], RZ.at[zid], m4.at[j], q4.at[zid], lead=2 * x + j, gx=x * 4 + j * 2 + core)

    def other(j):
        return jnp.logical_or(lead != 2 * x + j, zh != j)

    for j in range(2):

        @pl.when(other(j))
        def _():
            sum_z(j).start()

    def piece_to(k):
        return remote(S.at[(gx + k) % 16], RF.at[core], m5.at[k], q5.at[core], gx=(gx + k) % 16)

    @pl.when(builder)
    def _():
        F[pl.ds(0, 72), :] = A2[lead % 2]
        F[pl.ds(72, 8), :] = jnp.zeros((8, 128), F32)

        @pl.loop(1, 16)
        def _(k):
            src = (zid + k) % 16
            remote(A2.at[0], RZ.at[src], m4.at[0], q4.at[src], gx=gx).wait_recv()
            F[pl.ds(0, 72), :] += RZ[src]

        for h in range(2):

            @pl.when(core == h)
            def _():
                for to in range(16):
                    first = (9 * to - h + 1) // 2
                    S[to] = F[first : first + 8, :]

        RF[core] = S[gx]

        @pl.loop(1, 16)
        def _(k):
            piece_to(k).start()

    for c in range(2):

        @pl.when(jnp.logical_or(jnp.logical_not(builder), core != c))
        def _():
            remote(S.at[0], RF.at[c], m5.at[0], q5.at[c], gx=gx).wait_recv()

    even, odd = RF[core], RF[1 - core]
    for j in range(9):
        grad[j : j + 1, :] = (odd if j % 2 else even)[j // 2 : j // 2 + 1, :]

    across.wait_send()
    for up in (True, False):

        @pl.when(has[up])
        def _():
            halo(0, up).wait_send()
            halo(1, up).wait_send()

    for c in range(2):
        for y in range(2):

            @pl.when(is_other(c, y))
            def _():
                to_builder(c, y).wait_send()

    for k in range(1, 4):
        over_y(k, 0, True).wait_send()
        over_y(k, 1, True).wait_send()
        over_x(k, True).wait_send()
        sum_x(k).wait_send()
        sum_y(k).wait_send()
    for k in range(4):
        to_mate(k, True).wait_send()
    for m in range(CHUNKS):
        send_hidden(m).wait_send()
        send_grad(m).wait_send()
    for col, a, tap in taps:
        mate(tap).wait_send()
    for j in range(2):

        @pl.when(other(j))
        def _():
            sum_z(j).wait_send()

    @pl.when(builder)
    def _():
        @pl.loop(1, 16)
        def _(k):
            spread(k).wait_send()
            piece_to(k).wait_send()


def shards(inputs, lead_ids, film, flat_weights, cotangent):
    padded = jnp.pad(flat_weights.reshape(2, 9, 128), ((0, 0), (0, 7), (0, 0)))
    vmem = pl.BlockSpec(memory_space=pltpu.VMEM)
    outputs, total = pl.pallas_call(
        step_kernel,
        out_shape=(jax.ShapeDtypeStruct((512, 256), BF16), jax.ShapeDtypeStruct((9, 128), F32)),
        in_specs=[pl.BlockSpec(memory_space=pltpu.SMEM)] + [vmem] * 4,
        out_specs=(vmem, vmem),
        scratch_shapes=[
            pltpu.VMEM((2, 2, 2304, 128), BF16),
            pltpu.VMEM((2, 16, 16, 128), BF16),
            pltpu.VMEM((2, 3, 512, 256), BF16),
            pltpu.VMEM((2, 3, 256, 512), BF16),
            pltpu.VMEM((2, 512, 256), BF16),
            pltpu.VMEM((2, 512, 256), BF16),
            pltpu.VMEM((512, 256), BF16),
            pltpu.VMEM((512, 256), F32),
            pltpu.VMEM((512, 256), F32),
            pltpu.VMEM((2304, 128), F32),
            pltpu.VMEM((9, 256, 128), F32),
            pltpu.VMEM((9, 256, 128), F32),
            pltpu.VMEM((2304, 128), BF16),
            pltpu.VMEM((3, 576, 128), BF16),
            pltpu.VMEM((2, 4, 72, 128), F32),
            pltpu.VMEM((3, 2, 72, 128), F32),
            pltpu.VMEM((2, 72, 128), F32),
            pltpu.VMEM((16, 72, 128), F32),
            pltpu.VMEM((80, 128), F32),
            pltpu.VMEM((16, 8, 128), F32),
            pltpu.VMEM((2, 8, 128), F32),
            DMA((3, 2)), DMA((3, 2)),
            DMA((CHUNKS,)), DMA((CHUNKS,)),
            DMA((CHUNKS,)), DMA((CHUNKS,)),
            DMA((2, 2)), DMA((2, 16)),
            DMA((16,)), DMA((2,)),
            DMA((3, 2)), DMA((3, 2)),
            DMA((3,)), DMA((3,)),
            DMA((4,)), DMA((4,)),
            DMA((9,)), DMA((9,)),
            DMA((3,)), DMA((3,)),
            DMA((3,)), DMA((3,)),
            DMA((2,)), DMA((16,)),
            DMA((16,)), DMA((2,)),
        ],
        compiler_params=pltpu.CompilerParams(
            collective_id=0, has_side_effects=True, vmem_limit_bytes=50 << 20
        ),
    )(lead_ids, padded, inputs.reshape(512, 256), film, cotangent.reshape(512, 256))
    return (outputs.reshape(inputs.shape), total.reshape(-1))


def solution(mesh):
    return jax.shard_map(
        shards,
        mesh=mesh,
        in_specs=(
            P("lead", "gy", "gx", None),
            P("lead"),
            P(),
            P(None, ("lead", "gy", "gx")),
            P("lead", "gy", "gx", None),
        ),
        out_specs=(P("lead", "gy", "gx", None), P(("lead", "gy", "gx"))),
        check_vma=False,
    )
```

```python
import jax
import jax.numpy as jnp
from jax import lax
from jax.experimental import pallas as pl
from jax.experimental.pallas import tpu as pltpu
from jax.sharding import PartitionSpec as P

MESH = pl.DeviceIdType.MESH
DMA = pltpu.SemaphoreType.DMA
F32, BF16 = jnp.float32, jnp.bfloat16


def place():
    lead, gy, gx = lax.axis_index("lead"), lax.axis_index("gy"), lax.axis_index("gx")
    return lead, gy, gx, gx // 4, (gx // 2) % 2, gx % 2


def remote(src, dst, send_sem, recv_sem, **where):
    return pltpu.make_async_remote_copy(
        src_ref=src, dst_ref=dst, send_sem=send_sem, recv_sem=recv_sem, device_id=where, device_id_type=MESH
    )


def greet():
    lead, gy, gx, x, zh, core = place()
    barrier = pltpu.get_barrier_semaphore()
    first = gy - gy % 2

    def hello(**where):
        pl.semaphore_signal(barrier, inc=1, device_id=where, device_id_type=MESH)

    for k in (1, 15):
        hello(**ring(k))
    hello(gy=(gy + 2) % 4)
    hello(gy=3 - gy)
    for k in range(1, 16):
        hello(gy=first + (gy % 2 + k // 8) % 2, gx=(x + (k // 2) % 4) % 4 * 4 + zh * 2 + (core + k) % 2)
    pl.semaphore_wait(barrier, 19)


def ring(k):
    lead, gy, gx, x, zh, core = place()
    z = (zh * 8 + lead + k) % 16
    return {"lead": z % 8, "gx": x * 4 + (z // 8) * 2 + core}


ROWS = 128
CHUNKS = 4


def group(lead, gy):
    return pl.ds(pl.multiple_of((lead * 2 + gy // 2) * 144, 16), 144)


def quarter(x):
    return pl.ds(pl.multiple_of(x * 576, 64), 576)


def sigmoid(v):
    return 1.0 / (1.0 + jnp.exp(-v))


def step_kernel(
    ids, w_ref, x_hbm, film_hbm, cot_hbm, out, grad,
    W, R, BD, X, XT, H, GB, GA, DA, ACC, TA, TB, RC, T, RY, A2, PX, PP, ZB, ZR, RR, film, cot,
    ls, hs, hr, cs, cr, es, er, s1, r1, s2, r2, s3, r3, s4, r4, s5, r5, m1, q1, m2, q2, m3, q3, m4, q4, m5, q5,
):
    lead, gy, gx, x, zh, core = place()
    zid = zh * 8 + lead
    west = x // 2
    block = gy % 2
    pair = gy - block
    sent = []

    def finish():
        for wait in sent:
            wait()

    x_in = pltpu.make_async_copy(x_hbm, X.at[0, 1], ls.at[0])
    film_in = pltpu.make_async_copy(film_hbm, film, ls.at[1])
    cot_in = pltpu.make_async_copy(cot_hbm, cot, ls.at[2])
    x_in.start()
    film_in.start()
    cot_in.start()
    R[zh, lead] = w_ref[...]
    x_in.wait()
    greet()

    def hop(k, step):
        z = (zid + 16 - k * (step - 1)) % 16
        piece = R.at[z // 8, z % 8]
        way = (1 - k) // 2
        return remote(piece, piece, s1.at[way, step - 1], r1.at[way, step - 1], **ring(k % 16))

    def hop_in(k, step):
        z = (zid + 16 - k * step) % 16
        piece = R.at[z // 8, z % 8]
        way = (1 - k) // 2
        return remote(piece, piece, s1.at[way, step - 1], r1.at[way, step - 1], **ring(k % 16))

    hop(1, 1).start()
    hop(-1, 1).start()

    def halo(col, up):
        return remote(
            X.at[col, 1], X.at[col, 0 if up else 2], hs.at[col, int(up)], hr.at[col, int(up)],
            gy=(gy + (1 if up else 3)) % 4,
        )

    across = remote(X.at[0, 1], X.at[1, 1], hs.at[2, 0], hr.at[2, 0], gx=(gx + 8) % 16)
    has = {True: gy < 3, False: gy > 0}
    gets = {True: gy > 0, False: gy < 3}
    across.start()
    sent.append(across.wait_send)

    def halo_out(col):
        for up in (True, False):

            @pl.when(has[up])
            def _():
                halo(col, up).start()

    @sent.append
    def _():
        for col in range(2):
            for up in (True, False):

                @pl.when(has[up])
                def _():
                    halo(col, up).wait_send()

    def halo_in(col):
        for up in (True, False):

            @pl.when(gets[up])
            def _():
                halo(col, up).wait_recv()

            @pl.when(jnp.logical_not(gets[up]))
            def _():
                X[col, 0 if up else 2] = jnp.zeros((512, 256), BF16)

    halo_out(0)
    for step in range(1, 9):
        hop_in(1, step).wait_recv()
        if step < 8:
            hop(1, step + 1).start()
            hop_in(-1, step).wait_recv()
        if step < 7:
            hop(-1, step + 1).start()
        if step == 6:
            across.wait_recv()
            halo_out(1)

    @sent.append
    def _():
        for step in range(1, 9):
            hop(1, step).wait_send()
            if step < 8:
                hop(-1, step).wait_send()

    def gather(k):
        y, xx = (block + k // 8) % 2, (x + (k // 2) % 4) % 4
        return remote(
            R.at[:, pl.ds(2 * xx, 2), y], BD.at[block, x, core], s2.at[k], r2.at[block, x, core],
            gy=pair + y, gx=xx * 4 + zh * 2 + (core + k) % 2,
        )

    def gather_in(k):
        y, xx, c = (block + k // 8) % 2, (x + (k // 2) % 4) % 4, (core + k) % 2
        return remote(R.at[:, pl.ds(2 * x, 2), 0], BD.at[y, xx, c], s2.at[k], r2.at[y, xx, c], gy=gy, gx=gx)

    for k in range(1, 16):
        gather(k).start()
        sent.append(gather(k).wait_send)
    BD[block, x, core] = R[:, pl.ds(2 * x, 2), block]
    row = lax.broadcasted_iota(jnp.int32, (144, 512), 0) * 2 + core
    column = lax.broadcasted_iota(jnp.int32, (144, 512), 1)
    owner = (row * 57) >> 9
    place_of = ((owner >> 2) * 2 + (owner & 1)) * 2 + ((owner >> 1) & 1)
    pick = (column == place_of * 16 + (row - owner * 9)).astype(F32).astype(BF16)
    XT[0, 1] = X[0, 1].T
    for k in range(1, 16):
        gather_in(k).wait_recv()

    def needed(l, y):
        number = 2 * l + y // 2
        inside = ((number >= 1) & (number <= 3)) | ((number >= 7) & (number <= 8)) | ((number >= 12) & (number <= 14))
        return (y % 2 == 0) | inside

    def piece(l, y, sems, slot, **where):
        part = W.at[core, y % 2, group(l, y)]
        return remote(part, part, sems[0].at[slot], sems[1].at[slot], **where)

    def start_if(l, y, copy):
        @pl.when(needed(l, y))
        def _():
            copy.start()

        @sent.append
        def _():
            @pl.when(needed(l, y))
            def _():
                copy.wait_send()

    def wait_if(l, y, copy):
        @pl.when(needed(l, y))
        def _():
            copy.wait_recv()

    order = (1, 3, 2)

    def to_y(k):
        return {"gy": (gy + k) % 4}

    def to_x(k):
        return {"gx": (gx + 4 * k) % 16}

    for j in range(2):
        W[core, block, group(2 * x + j, gy), :] = jnp.dot(
            pick, BD[:, :, :, :, j].reshape(512, 128), preferred_element_type=F32
        ).astype(BF16)
        for k in order:
            l = 2 * x + j
            start_if(l, gy, piece(l, gy, (s3, r3), (j, k - 1), **(to_x(k) if j else to_y(k))))
        for k in order:
            l = 2 * x + j
            start_if(l, gy, piece(l, gy, (s4, r4), (j, 0, k - 1), **(to_y(k) if j else to_x(k))))
    XT[1, 1] = X[1, 1].T
    for n in order:
        for j in range(2):
            l, y = (2 * ((x + 4 - n) % 4) + 1, gy) if j else (2 * x, (gy + 4 - n) % 4)
            wait_if(l, y, piece(l, y, (s3, r3), (j, n - 1), gx=gx))
            for k in order:
                start_if(l, y, piece(l, y, (s4, r4), (j, n, k - 1), **(to_y(k) if j else to_x(k))))
    for col in range(2):
        halo_in(col)
        for a in (0, 2):
            XT[col, a] = X[col, a].T
    for tap in range(3):
        at = pl.ds(pl.multiple_of((3 * tap + 2 * west) * 256, 256), 256)
        TA[at, :] = jnp.zeros((256, 128), F32)
        RC[at, :] = jnp.zeros((256, 128), F32)
    for n in (0,) + order:
        for k in order:
            for j in range(2):
                if j:
                    l, y = 2 * ((x + 4 - n) % 4) + 1, (gy + 4 - k) % 4
                else:
                    l, y = 2 * ((x + 4 - k) % 4), (gy + 4 - n) % 4
                wait_if(l, y, piece(l, y, (s4, r4), (j, n, k - 1), gx=gx))

    def to_mate(part, start):
        h = core if start else 1 - core
        rows = pl.ds(0, 2304) if part == 0 else pl.ds(256 + 768 * (part - 1), 256)
        view = W.at[h, min(part, 1), rows]
        return remote(view, view, s5.at[part], r5.at[part], gx=gx + 1 - 2 * core)

    for part in range(4):
        to_mate(part, True).start()
        sent.append(to_mate(part, True).wait_send)
    film_in.wait()
    cot_in.wait()
    to_mate(0, False).wait_recv()

    row = film[ids[0]]
    mult_a, shift_a, mult_b, shift_b = 1.0 + row[0:1], row[1:2], 1.0 + row[2:3], row[3:4]

    def half(h, block, tap):
        return W[h, block, pl.ds(pl.multiple_of(tap * 256, 256), 256), :]

    def weight(block, tap):
        return jnp.concatenate([half(0, block, tap), half(1, block, tap)], axis=1)

    taps = [(0, 1, 1 + 3), (0, 0, 1), (0, 2, 7)] + [(1, a, 3 * a + 2 - 2 * west) for a in (1, 0, 2)]

    def rows_of(m):
        return pl.ds(pl.multiple_of(m * ROWS, ROWS), ROWS)

    def send_hidden(m):
        return remote(H.at[0, rows_of(m)], H.at[1, rows_of(m)], cs.at[m], cr.at[m], gy=(gy + 2) % 4)

    @pl.loop(0, CHUNKS)
    def _(m):
        r = rows_of(m)
        pre = jnp.zeros((ROWS, 256), F32)
        for col, a, tap in taps:
            pre = pre + jnp.dot(X[col, a, r, :], weight(0, tap), preferred_element_type=F32)
        pre = pre * mult_a + shift_a
        sig = sigmoid(pre)
        H[0, r, :] = (X[0, 1, r, :].astype(F32) + pre * sig).astype(BF16)
        DA[r, :] = mult_a * sig * (1.0 + pre * (1.0 - sig))
        send_hidden(m).start()

    @sent.append
    def _():
        @pl.loop(0, CHUNKS)
        def _(m):
            send_hidden(m).wait_send()
            send_grad(m).wait_send()

    for part in range(1, 4):
        to_mate(part, False).wait_recv()
    south = gy // 2

    @pl.loop(0, CHUNKS)
    def _(m):
        r = rows_of(m)
        ACC[r, :] = jnp.dot(H[0, r, :], weight(1, 4), preferred_element_type=F32)

    def send_grad(m):
        return remote(GB.at[0, rows_of(m)], GB.at[1, rows_of(m)], es.at[m], er.at[m], gy=(gy + 2) % 4)

    @pl.loop(0, CHUNKS)
    def _(m):
        r = rows_of(m)
        send_hidden(m).wait_recv()
        pre = ACC[r, :] + jnp.dot(H[1, r, :], weight(1, 7 - 6 * south), preferred_element_type=F32)
        pre = pre * mult_b + shift_b
        sig = sigmoid(pre)
        up = cot[r, :].astype(F32)
        GB[0, r, :] = (up * mult_b * sig * (1.0 + pre * (1.0 - sig))).astype(BF16)
        send_grad(m).start()
        out[r, :] = (H[0, r, :].astype(F32) + pre * sig).astype(BF16)

    def back_dot(value, tap):
        turned = (((1,), (1,)), ((), ()))
        return lax.dot_general(
            value[:, :128], half(0, 1, tap), turned, preferred_element_type=F32
        ) + lax.dot_general(value[:, 128:], half(1, 1, tap), turned, preferred_element_type=F32)

    @pl.loop(0, CHUNKS)
    def _(m):
        r = rows_of(m)
        ACC[r, :] = cot[r, :].astype(F32) + back_dot(GB[0, r, :], 4)

    @pl.loop(0, CHUNKS)
    def _(m):
        r = rows_of(m)
        send_grad(m).wait_recv()
        back = ACC[r, :] + back_dot(GB[1, r, :], 1 + 6 * south)
        value = back * DA[r, :]
        left, right = value[:, :128], value[:, 128:]
        GA[r, :] = jnp.concatenate(
            [jnp.where(core == 0, left, right), jnp.where(core == 0, right, left)], axis=1
        ).astype(BF16)

    scale = 1.0 / 512.0

    def mate(tap):
        at = pl.ds(pl.multiple_of(tap * 256, 256), 256)
        return remote(TB.at[at], RC.at[at], m1.at[tap], q1.at[tap], gx=gx + 1 - 2 * core)

    for col, a, tap in taps:
        at = pl.ds(pl.multiple_of(tap * 256, 256), 256)
        term = jnp.dot(XT[col, a], GA[...], preferred_element_type=F32) * scale
        TB[at, :] = term[:, 128:]
        mate(tap).start()
        sent.append(mate(tap).wait_send)
        TA[at, :] = term[:, :128]
    for col, a, tap in taps:
        mate(tap).wait_recv()

    def rows72(l, y):
        return pl.ds(pl.multiple_of((l * 4 + y) * 72, 8), 72)

    def sum_y(k):
        return remote(T.at[k - 1], RY.at[k - 1], m2.at[k - 1], q2.at[k - 1], gy=(gy + k) % 4)

    for k in order:

        @pl.loop(0, 8)
        def _(l):
            at = rows72(l, (gy + k) % 4)
            T[k - 1, l] = (TA[at, :] + RC[at, :]).astype(BF16)

        sum_y(k).start()
        sent.append(sum_y(k).wait_send)
    for k in order:
        sum_y(k).wait_recv()

    @pl.loop(0, 8)
    def _(l):
        at = rows72(l, gy)
        A2[l] = TA[at, :] + RC[at, :] + RY[0, l].astype(F32) + RY[1, l].astype(F32) + RY[2, l].astype(F32)

    def window(xx):
        return A2.at[:, pl.ds(pl.multiple_of(xx * 16, 16), 24)]

    def sum_x(k):
        return remote(window((x + k) % 4), PX.at[k - 1], m3.at[k - 1], q3.at[k - 1], gx=(gx + 4 * k) % 16)

    for k in order:
        sum_x(k).start()
        sent.append(sum_x(k).wait_send)
    for k in order:
        sum_x(k).wait_recv()
    P = A2[:, pl.ds(pl.multiple_of(x * 16, 16), 24), :] + PX[0] + PX[1] + PX[2]
    PP[...] = P
    ZB[0] = P[:, 0:16].astype(BF16)
    ZB[1] = P[:, 8:24].astype(BF16)

    def sum_z(k):
        z = (zid + k) % 16
        return remote(ZB.at[z // 8, z % 8], ZR.at[k], m4.at[k], q4.at[k], **ring(k))

    far_first = (8, 7, 9, 6, 10, 5, 11, 4, 12, 3, 13, 2, 14, 1, 15)
    for k in far_first:
        sum_z(k).start()
        sent.append(sum_z(k).wait_send)
    total = PP[lead, pl.ds(pl.multiple_of(zh * 8, 8), 16), :]
    for k in far_first[::-1]:
        sum_z(k).wait_recv()
        total = total + ZR[k].astype(F32)
    RR[core] = total
    swap = remote(RR.at[core], RR.at[core], m5, q5, gx=gx + 1 - 2 * core)
    swap_in = remote(RR.at[1 - core], RR.at[1 - core], m5, q5, gx=gx + 1 - 2 * core)
    swap.start()
    sent.append(swap.wait_send)
    swap_in.wait_recv()
    for j in range(9):
        grad[j : j + 1, :] = RR[(j + core) % 2, pl.ds(2 * x + zh + (9 * core + j) // 2, 1), :]
    finish()


def shards(inputs, lead_ids, film, flat_weights, cotangent):
    padded = jnp.pad(flat_weights.reshape(2, 9, 128), ((0, 0), (0, 7), (0, 0)))
    vmem = pl.BlockSpec(memory_space=pltpu.VMEM)
    hbm = pl.BlockSpec(memory_space=pltpu.HBM)
    outputs, total = pl.pallas_call(
        step_kernel,
        out_shape=(jax.ShapeDtypeStruct((512, 256), BF16), jax.ShapeDtypeStruct((9, 128), F32)),
        in_specs=[pl.BlockSpec(memory_space=pltpu.SMEM), vmem, hbm, hbm, hbm],
        out_specs=(vmem, vmem),
        scratch_shapes=[
            pltpu.VMEM((2, 2, 2304, 128), BF16),
            pltpu.VMEM((2, 8, 2, 16, 128), BF16),
            pltpu.VMEM((2, 4, 2, 2, 2, 16, 128), BF16),
            pltpu.VMEM((2, 3, 512, 256), BF16),
            pltpu.VMEM((2, 3, 256, 512), BF16),
            pltpu.VMEM((2, 512, 256), BF16),
            pltpu.VMEM((2, 512, 256), BF16),
            pltpu.VMEM((512, 256), BF16),
            pltpu.VMEM((512, 256), F32),
            pltpu.VMEM((512, 256), F32),
            pltpu.VMEM((2304, 128), F32),
            pltpu.VMEM((2304, 128), F32),
            pltpu.VMEM((2304, 128), F32),
            pltpu.VMEM((3, 8, 72, 128), BF16),
            pltpu.VMEM((3, 8, 72, 128), BF16),
            pltpu.VMEM((8, 72, 128), F32),
            pltpu.VMEM((3, 8, 24, 128), F32),
            pltpu.VMEM((8, 24, 128), F32),
            pltpu.VMEM((2, 8, 16, 128), BF16),
            pltpu.VMEM((16, 16, 128), BF16),
            pltpu.VMEM((2, 16, 128), F32),
            pltpu.VMEM((360, 4, 256), F32),
            pltpu.VMEM((512, 256), BF16),
            DMA((3,)),
            DMA((3, 2)), DMA((3, 2)),
            DMA((CHUNKS,)), DMA((CHUNKS,)),
            DMA((CHUNKS,)), DMA((CHUNKS,)),
            DMA((2, 8)), DMA((2, 8)),
            DMA((16,)), DMA((2, 4, 2)),
            DMA((2, 3)), DMA((2, 3)),
            DMA((2, 4, 3)), DMA((2, 4, 3)),
            DMA((4,)), DMA((4,)),
            DMA((9,)), DMA((9,)),
            DMA((3,)), DMA((3,)),
            DMA((3,)), DMA((3,)),
            DMA((16,)), DMA((16,)),
            DMA(()), DMA(()),
        ],
        compiler_params=pltpu.CompilerParams(
            collective_id=0, has_side_effects=True, vmem_limit_bytes=50 << 20
        ),
    )(lead_ids, padded, inputs.reshape(512, 256), film, cotangent.reshape(512, 256))
    return (outputs.reshape(inputs.shape), total.reshape(-1))


def solution(mesh):
    return jax.shard_map(
        shards,
        mesh=mesh,
        in_specs=(
            P("lead", "gy", "gx", None),
            P("lead"),
            P(),
            P(None, ("lead", "gy", "gx")),
            P("lead", "gy", "gx", None),
        ),
        out_specs=(P("lead", "gy", "gx", None), P(("lead", "gy", "gx"))),
        check_vma=False,
    )
```

```python
import jax
import jax.numpy as jnp
from jax import lax
from jax.experimental import pallas as pl
from jax.experimental.pallas import tpu as pltpu
from jax.sharding import PartitionSpec as P

MESH = pl.DeviceIdType.MESH
DMA = pltpu.SemaphoreType.DMA
F32, BF16 = jnp.float32, jnp.bfloat16


def place():
    lead, gy, gx = lax.axis_index("lead"), lax.axis_index("gy"), lax.axis_index("gx")
    return lead, gy, gx, gx // 4, (gx // 2) % 2, gx % 2


def remote(src, dst, send_sem, recv_sem, **where):
    return pltpu.make_async_remote_copy(
        src_ref=src, dst_ref=dst, send_sem=send_sem, recv_sem=recv_sem, device_id=where, device_id_type=MESH
    )


def greet():
    lead, gy, gx, x, zh, core = place()
    barrier = pltpu.get_barrier_semaphore()
    first = gy - gy % 2

    def hello(**where):
        pl.semaphore_signal(barrier, inc=1, device_id=where, device_id_type=MESH)

    for k in range(1, 16):
        hello(**ring(k))
    hello(gy=(gy + 2) % 4)
    hello(gy=3 - gy)
    for k in range(1, 16):
        hello(gy=first + (gy % 2 + k // 8) % 2, gx=(x + (k // 2) % 4) % 4 * 4 + zh * 2 + (core + k) % 2)
    pl.semaphore_wait(barrier, 32)


def ring(k):
    lead, gy, gx, x, zh, core = place()
    z = (zh * 8 + lead + k) % 16
    return {"lead": z % 8, "gx": x * 4 + (z // 8) * 2 + core}


ROWS = 128
CHUNKS = 4


def group(lead, gy):
    return pl.ds(pl.multiple_of((lead * 2 + gy // 2) * 144, 16), 144)


def quarter(x):
    return pl.ds(pl.multiple_of(x * 576, 64), 576)


def sigmoid(v):
    return 1.0 / (1.0 + jnp.exp(-v))


def step_kernel(
    ids, w_ref, x_hbm, film_hbm, cot_hbm, out, grad,
    W, R, BD, X, XT, H, GB, GA, DA, ACC, TA, TB, RC, T, RY, A2, XB, PX, PP, ZB, ZR, RR, film, cot,
    ls, hs, hr, cs, cr, es, er, s1, r1, s2, r2, s3, r3, s4, r4, s5, r5, m1, q1, m2, q2, m3, q3, m4, q4, m5, q5,
):
    lead, gy, gx, x, zh, core = place()
    zid = zh * 8 + lead
    west = x // 2
    block = gy % 2
    pair = gy - block
    sent = []

    def finish():
        for wait in sent:
            wait()

    x_in = pltpu.make_async_copy(x_hbm, X.at[0, 1], ls.at[0])
    film_in = pltpu.make_async_copy(film_hbm, film, ls.at[1])
    cot_in = pltpu.make_async_copy(cot_hbm, cot, ls.at[2])
    x_in.start()
    film_in.start()
    cot_in.start()
    R[zh, lead] = w_ref[...]
    x_in.wait()
    greet()

    far_first = (8, 7, 9, 6, 10, 5, 11, 4, 12, 3, 13, 2, 14, 1, 15)

    def needed(l, y):
        number = 2 * l + y // 2
        inside = ((number >= 1) & (number <= 3)) | ((number >= 7) & (number <= 8)) | ((number >= 12) & (number <= 14))
        return (y % 2 == 0) | inside

    def spread(k, blk):
        own = R.at[zh, lead, blk]
        return remote(own, own, s1.at[blk, k], r1.at[blk, k], **ring(k))

    def spread_in(k, blk):
        z = (zid + 16 - k) % 16
        own = R.at[z // 8, z % 8, blk]
        return remote(own, own, s1.at[blk, k], r1.at[blk, k], **ring(k))

    for k in far_first:
        spread(k, 0).start()

    @pl.when(needed(lead, pair + 1))
    def _():
        for k in far_first:
            spread(k, 1).start()

    @sent.append
    def _():
        for k in far_first:
            spread(k, 0).wait_send()

        @pl.when(needed(lead, pair + 1))
        def _():
            for k in far_first:
                spread(k, 1).wait_send()

    def halo(col, up):
        return remote(
            X.at[col, 1], X.at[col, 0 if up else 2], hs.at[col, int(up)], hr.at[col, int(up)],
            gy=(gy + (1 if up else 3)) % 4,
        )

    def across(part):
        rows = pl.ds(256 * part, 256)
        return remote(X.at[0, 1, rows], X.at[1, 1, rows], hs.at[2, part], hr.at[2, part], gx=(gx + 8) % 16)

    def corner(part, up):
        rows = pl.ds(256 * part, 256)
        return remote(
            X.at[1, 1, rows], X.at[1, 0 if up else 2, rows], hs.at[1 + 2 * part, int(up)], hr.at[1 + 2 * part, int(up)],
            gy=(gy + (1 if up else 3)) % 4,
        )

    has = {True: gy < 3, False: gy > 0}
    gets = {True: gy > 0, False: gy < 3}
    for part in range(2):
        across(part).start()
        sent.append(across(part).wait_send)

    def halo_out():
        for up in (True, False):

            @pl.when(has[up])
            def _():
                halo(0, up).start()

    def corner_out(part):
        across(part).wait_recv()
        for up in (True, False):

            @pl.when(has[up])
            def _():
                corner(part, up).start()

    @sent.append
    def _():
        for up in (True, False):

            @pl.when(has[up])
            def _():
                halo(0, up).wait_send()
                corner(0, up).wait_send()
                corner(1, up).wait_send()

    def halo_in(col):
        for up in (True, False):

            @pl.when(gets[up])
            def _():
                if col == 0:
                    halo(0, up).wait_recv()
                else:
                    corner(0, up).wait_recv()
                    corner(1, up).wait_recv()

            @pl.when(jnp.logical_not(gets[up]))
            def _():
                X[col, 0 if up else 2] = jnp.zeros((512, 256), BF16)

    halo_out()
    corner_out(0)
    XT[0, 1] = X[0, 1].T
    for k in far_first[::-1]:
        spread_in(k, 0).wait_recv()
        z = (zid + 16 - k) % 16

        @pl.when(needed(z % 8, pair + 1))
        def _():
            spread_in(k, 1).wait_recv()

    def gather(k):
        y, xx = (block + k // 8) % 2, (x + (k // 2) % 4) % 4
        return remote(
            R.at[:, pl.ds(2 * xx, 2), y], BD.at[block, x, core], s2.at[k], r2.at[block, x, core],
            gy=pair + y, gx=xx * 4 + zh * 2 + (core + k) % 2,
        )

    def gather_in(k):
        y, xx, c = (block + k // 8) % 2, (x + (k // 2) % 4) % 4, (core + k) % 2
        return remote(R.at[:, pl.ds(2 * x, 2), 0], BD.at[y, xx, c], s2.at[k], r2.at[y, xx, c], gy=gy, gx=gx)

    for k in range(1, 16):
        gather(k).start()
        sent.append(gather(k).wait_send)
    BD[block, x, core] = R[:, pl.ds(2 * x, 2), block]
    row = lax.broadcasted_iota(jnp.int32, (144, 512), 0) * 2 + core
    column = lax.broadcasted_iota(jnp.int32, (144, 512), 1)
    owner = (row * 57) >> 9
    place_of = ((owner >> 2) * 2 + (owner & 1)) * 2 + ((owner >> 1) & 1)
    pick = (column == place_of * 16 + (row - owner * 9)).astype(F32).astype(BF16)
    corner_out(1)
    for k in range(1, 16):
        gather_in(k).wait_recv()

    def piece(l, y, sems, slot, **where):
        part = W.at[core, y % 2, group(l, y)]
        return remote(part, part, sems[0].at[slot], sems[1].at[slot], **where)

    def start_if(l, y, copy):
        @pl.when(needed(l, y))
        def _():
            copy.start()

        @sent.append
        def _():
            @pl.when(needed(l, y))
            def _():
                copy.wait_send()

    def wait_if(l, y, copy):
        @pl.when(needed(l, y))
        def _():
            copy.wait_recv()

    order = (1, 3, 2)

    def to_y(k):
        return {"gy": (gy + k) % 4}

    def to_x(k):
        return {"gx": (gx + 4 * k) % 16}

    for j in range(2):
        W[core, block, group(2 * x + j, gy), :] = jnp.dot(
            pick, BD[:, :, :, :, j].reshape(512, 128), preferred_element_type=F32
        ).astype(BF16)
        for k in order:
            l = 2 * x + j
            start_if(l, gy, piece(l, gy, (s3, r3), (j, k - 1), **(to_x(k) if j else to_y(k))))
        for k in order:
            l = 2 * x + j
            start_if(l, gy, piece(l, gy, (s4, r4), (j, 0, k - 1), **(to_y(k) if j else to_x(k))))
    XT[1, 1] = X[1, 1].T
    for n in order:
        for j in range(2):
            l, y = (2 * ((x + 4 - n) % 4) + 1, gy) if j else (2 * x, (gy + 4 - n) % 4)
            wait_if(l, y, piece(l, y, (s3, r3), (j, n - 1), gx=gx))
            for k in order:
                start_if(l, y, piece(l, y, (s4, r4), (j, n, k - 1), **(to_y(k) if j else to_x(k))))
    for col in range(2):
        halo_in(col)
        for a in (0, 2):
            XT[col, a] = X[col, a].T
    for tap in range(3):
        at = pl.ds(pl.multiple_of((3 * tap + 2 * west) * 256, 256), 256)
        TA[at, :] = jnp.zeros((256, 128), F32)
        RC[at, :] = jnp.zeros((256, 128), F32)
    for n in (0,) + order:
        for k in order:
            for j in range(2):
                if j:
                    l, y = 2 * ((x + 4 - n) % 4) + 1, (gy + 4 - k) % 4
                else:
                    l, y = 2 * ((x + 4 - k) % 4), (gy + 4 - n) % 4
                wait_if(l, y, piece(l, y, (s4, r4), (j, n, k - 1), gx=gx))

    def to_mate(part, start):
        h = core if start else 1 - core
        rows = pl.ds(0, 2304) if part == 0 else pl.ds(256 + 768 * (part - 1), 256)
        view = W.at[h, min(part, 1), rows]
        return remote(view, view, s5.at[part], r5.at[part], gx=gx + 1 - 2 * core)

    for part in range(4):
        to_mate(part, True).start()
        sent.append(to_mate(part, True).wait_send)
    film_in.wait()
    cot_in.wait()
    to_mate(0, False).wait_recv()

    row = film[ids[0]]
    mult_a, shift_a, mult_b, shift_b = 1.0 + row[0:1], row[1:2], 1.0 + row[2:3], row[3:4]

    def half(h, block, tap):
        return W[h, block, pl.ds(pl.multiple_of(tap * 256, 256), 256), :]

    def weight(block, tap):
        return jnp.concatenate([half(0, block, tap), half(1, block, tap)], axis=1)

    taps = [(0, 1, 1 + 3), (0, 0, 1), (0, 2, 7)] + [(1, a, 3 * a + 2 - 2 * west) for a in (1, 0, 2)]

    def rows_of(m):
        return pl.ds(pl.multiple_of(m * ROWS, ROWS), ROWS)

    def send_hidden(m):
        return remote(H.at[0, rows_of(m)], H.at[1, rows_of(m)], cs.at[m], cr.at[m], gy=(gy + 2) % 4)

    @pl.loop(0, CHUNKS)
    def _(m):
        r = rows_of(m)
        pre = jnp.zeros((ROWS, 256), F32)
        for col, a, tap in taps:
            pre = pre + jnp.dot(X[col, a, r, :], weight(0, tap), preferred_element_type=F32)
        pre = pre * mult_a + shift_a
        sig = sigmoid(pre)
        H[0, r, :] = (X[0, 1, r, :].astype(F32) + pre * sig).astype(BF16)
        DA[r, :] = mult_a * sig * (1.0 + pre * (1.0 - sig))
        send_hidden(m).start()

    @sent.append
    def _():
        @pl.loop(0, CHUNKS)
        def _(m):
            send_hidden(m).wait_send()
            send_grad(m).wait_send()

    for part in range(1, 4):
        to_mate(part, False).wait_recv()
    south = gy // 2

    @pl.loop(0, CHUNKS)
    def _(m):
        r = rows_of(m)
        ACC[r, :] = jnp.dot(H[0, r, :], weight(1, 4), preferred_element_type=F32)

    def send_grad(m):
        return remote(GB.at[0, rows_of(m)], GB.at[1, rows_of(m)], es.at[m], er.at[m], gy=(gy + 2) % 4)

    @pl.loop(0, CHUNKS)
    def _(m):
        r = rows_of(m)
        send_hidden(m).wait_recv()
        pre = ACC[r, :] + jnp.dot(H[1, r, :], weight(1, 7 - 6 * south), preferred_element_type=F32)
        pre = pre * mult_b + shift_b
        sig = sigmoid(pre)
        up = cot[r, :].astype(F32)
        GB[0, r, :] = (up * mult_b * sig * (1.0 + pre * (1.0 - sig))).astype(BF16)
        send_grad(m).start()
        out[r, :] = (H[0, r, :].astype(F32) + pre * sig).astype(BF16)

    def back_dot(value, tap):
        turned = (((1,), (1,)), ((), ()))
        return lax.dot_general(
            value[:, :128], half(0, 1, tap), turned, preferred_element_type=F32
        ) + lax.dot_general(value[:, 128:], half(1, 1, tap), turned, preferred_element_type=F32)

    @pl.loop(0, CHUNKS)
    def _(m):
        r = rows_of(m)
        ACC[r, :] = cot[r, :].astype(F32) + back_dot(GB[0, r, :], 4)

    @pl.loop(0, CHUNKS)
    def _(m):
        r = rows_of(m)
        send_grad(m).wait_recv()
        back = ACC[r, :] + back_dot(GB[1, r, :], 1 + 6 * south)
        value = back * DA[r, :]
        left, right = value[:, :128], value[:, 128:]
        GA[r, :] = jnp.concatenate(
            [jnp.where(core == 0, left, right), jnp.where(core == 0, right, left)], axis=1
        ).astype(BF16)

    scale = 1.0 / 512.0

    def mate(tap):
        at = pl.ds(pl.multiple_of(tap * 256, 256), 256)
        return remote(TB.at[at], RC.at[at], m1.at[tap], q1.at[tap], gx=gx + 1 - 2 * core)

    for col, a, tap in taps:
        at = pl.ds(pl.multiple_of(tap * 256, 256), 256)
        term = jnp.dot(XT[col, a], GA[...], preferred_element_type=F32) * scale
        TB[at, :] = term[:, 128:]
        mate(tap).start()
        sent.append(mate(tap).wait_send)
        TA[at, :] = term[:, :128]
    for col, a, tap in taps:
        mate(tap).wait_recv()

    def rows72(l, y):
        return pl.ds(pl.multiple_of((l * 4 + y) * 72, 8), 72)

    def empty(l, y):
        number = 4 * l + y
        first = ((number >= 0) & (number <= 2)) | ((number >= 11) & (number <= 13)) | ((number >= 22) & (number <= 23))
        last = ((number >= 8) & (number <= 9)) | ((number >= 18) & (number <= 20)) | (number >= 29)
        return ((west == 0) & first) | ((west == 1) & last)

    def sum_y(k, l):
        return remote(T.at[k - 1, l], RY.at[k - 1, l], m2.at[k - 1, l], q2.at[k - 1, l], gy=(gy + k) % 4)

    for k in order:

        @pl.loop(0, 8)
        def _(l):
            at = rows72(l, (gy + k) % 4)

            @pl.when(jnp.logical_not(empty(l, (gy + k) % 4)))
            def _():
                T[k - 1, l] = (TA[at, :] + RC[at, :]).astype(BF16)
                sum_y(k, l).start()

    @sent.append
    def _():
        for k in order:

            @pl.loop(0, 8)
            def _(l):
                @pl.when(jnp.logical_not(empty(l, (gy + k) % 4)))
                def _():
                    sum_y(k, l).wait_send()

    @pl.loop(0, 8)
    def _(l):
        at = rows72(l, gy)
        A2[l] = TA[at, :] + RC[at, :]

    for k in order:

        @pl.loop(0, 8)
        def _(l):
            @pl.when(jnp.logical_not(empty(l, gy)))
            def _():
                sum_y(k, l).wait_recv()
                A2[l] += RY[k - 1, l].astype(F32)

    def sum_x(k):
        return remote(XB.at[k - 1], PX.at[k - 1], m3.at[k - 1], q3.at[k - 1], gx=(gx + 4 * k) % 16)

    def window(xx):
        return A2[:, pl.ds(pl.multiple_of(xx * 16, 16), 24), :]

    for k in order:
        XB[k - 1] = window((x + k) % 4).astype(BF16)
        sum_x(k).start()
        sent.append(sum_x(k).wait_send)
    PP[...] = window(x)
    for k in order:
        sum_x(k).wait_recv()
    P = PP[...] + PX[0].astype(F32) + PX[1].astype(F32) + PX[2].astype(F32)
    PP[...] = P
    ZB[0] = P[:, 0:16].astype(BF16)
    ZB[1] = P[:, 8:24].astype(BF16)

    def sum_z(k):
        z = (zid + k) % 16
        return remote(ZB.at[z // 8, z % 8], ZR.at[k], m4.at[k], q4.at[k], **ring(k))

    for k in far_first:
        sum_z(k).start()
        sent.append(sum_z(k).wait_send)
    total = PP[lead, pl.ds(pl.multiple_of(zh * 8, 8), 16), :]
    for k in far_first[::-1]:
        sum_z(k).wait_recv()
        total = total + ZR[k].astype(F32)
    RR[core] = total
    swap = remote(RR.at[core], RR.at[core], m5, q5, gx=gx + 1 - 2 * core)
    swap_in = remote(RR.at[1 - core], RR.at[1 - core], m5, q5, gx=gx + 1 - 2 * core)
    swap.start()
    sent.append(swap.wait_send)
    swap_in.wait_recv()
    for j in range(9):
        grad[j : j + 1, :] = RR[(j + core) % 2, pl.ds(2 * x + zh + (9 * core + j) // 2, 1), :]
    finish()


def shards(inputs, lead_ids, film, flat_weights, cotangent):
    padded = jnp.pad(flat_weights.reshape(2, 9, 128), ((0, 0), (0, 7), (0, 0)))
    vmem = pl.BlockSpec(memory_space=pltpu.VMEM)
    hbm = pl.BlockSpec(memory_space=pltpu.HBM)
    outputs, total = pl.pallas_call(
        step_kernel,
        out_shape=(jax.ShapeDtypeStruct((512, 256), BF16), jax.ShapeDtypeStruct((9, 128), F32)),
        in_specs=[pl.BlockSpec(memory_space=pltpu.SMEM), vmem, hbm, hbm, hbm],
        out_specs=(vmem, vmem),
        scratch_shapes=[
            pltpu.VMEM((2, 2, 2304, 128), BF16),
            pltpu.VMEM((2, 8, 2, 16, 128), BF16),
            pltpu.VMEM((2, 4, 2, 2, 2, 16, 128), BF16),
            pltpu.VMEM((2, 3, 512, 256), BF16),
            pltpu.VMEM((2, 3, 256, 512), BF16),
            pltpu.VMEM((2, 512, 256), BF16),
            pltpu.VMEM((2, 512, 256), BF16),
            pltpu.VMEM((512, 256), BF16),
            pltpu.VMEM((512, 256), F32),
            pltpu.VMEM((512, 256), F32),
            pltpu.VMEM((2304, 128), F32),
            pltpu.VMEM((2304, 128), F32),
            pltpu.VMEM((2304, 128), F32),
            pltpu.VMEM((3, 8, 72, 128), BF16),
            pltpu.VMEM((3, 8, 72, 128), BF16),
            pltpu.VMEM((8, 72, 128), F32),
            pltpu.VMEM((3, 8, 24, 128), BF16),
            pltpu.VMEM((3, 8, 24, 128), BF16),
            pltpu.VMEM((8, 24, 128), F32),
            pltpu.VMEM((2, 8, 16, 128), BF16),
            pltpu.VMEM((16, 16, 128), BF16),
            pltpu.VMEM((2, 16, 128), F32),
            pltpu.VMEM((360, 4, 256), F32),
            pltpu.VMEM((512, 256), BF16),
            DMA((3,)),
            DMA((4, 2)), DMA((4, 2)),
            DMA((CHUNKS,)), DMA((CHUNKS,)),
            DMA((CHUNKS,)), DMA((CHUNKS,)),
            DMA((2, 16)), DMA((2, 16)),
            DMA((16,)), DMA((2, 4, 2)),
            DMA((2, 3)), DMA((2, 3)),
            DMA((2, 4, 3)), DMA((2, 4, 3)),
            DMA((4,)), DMA((4,)),
            DMA((9,)), DMA((9,)),
            DMA((3, 8)), DMA((3, 8)),
            DMA((3,)), DMA((3,)),
            DMA((16,)), DMA((16,)),
            DMA(()), DMA(()),
        ],
        compiler_params=pltpu.CompilerParams(
            collective_id=0, has_side_effects=True, vmem_limit_bytes=50 << 20
        ),
    )(lead_ids, padded, inputs.reshape(512, 256), film, cotangent.reshape(512, 256))
    return (outputs.reshape(inputs.shape), total.reshape(-1))


def solution(mesh):
    return jax.shard_map(
        shards,
        mesh=mesh,
        in_specs=(
            P("lead", "gy", "gx", None),
            P("lead"),
            P(),
            P(None, ("lead", "gy", "gx")),
            P("lead", "gy", "gx", None),
        ),
        out_specs=(P("lead", "gy", "gx", None), P(("lead", "gy", "gx"))),
        check_vma=False,
    )
```

```python
import jax
import jax.numpy as jnp
from jax import lax
from jax.experimental import pallas as pl
from jax.experimental.pallas import tpu as pltpu
from jax.sharding import PartitionSpec as P

MESH = pl.DeviceIdType.MESH
DMA = pltpu.SemaphoreType.DMA
F32, BF16 = jnp.float32, jnp.bfloat16


def place():
    lead, gy, gx = lax.axis_index("lead"), lax.axis_index("gy"), lax.axis_index("gx")
    return lead, gy, gx, gx // 4, (gx // 2) % 2, gx % 2


def remote(src, dst, send_sem, recv_sem, **where):
    return pltpu.make_async_remote_copy(
        src_ref=src, dst_ref=dst, send_sem=send_sem, recv_sem=recv_sem, device_id=where, device_id_type=MESH
    )


def greet():
    lead, gy, gx, x, zh, core = place()
    barrier = pltpu.get_barrier_semaphore()
    first = gy - gy % 2

    def hello(**where):
        pl.semaphore_signal(barrier, inc=1, device_id=where, device_id_type=MESH)

    for k in range(1, 16):
        hello(**ring(k))
    hello(gy=(gy + 2) % 4)
    hello(gy=3 - gy)
    for k in range(1, 16):
        hello(gy=first + (gy % 2 + k // 8) % 2, gx=(x + (k // 2) % 4) % 4 * 4 + zh * 2 + (core + k) % 2)
    pl.semaphore_wait(barrier, 32)


def ring(k):
    lead, gy, gx, x, zh, core = place()
    z = (zh * 8 + lead + k) % 16
    return {"lead": z % 8, "gx": x * 4 + (z // 8) * 2 + core}


ROWS = 128
CHUNKS = 4


def group(lead, gy):
    return pl.ds(pl.multiple_of((lead * 2 + gy // 2) * 144, 16), 144)


def quarter(x):
    return pl.ds(pl.multiple_of(x * 576, 64), 576)


def sigmoid(v):
    return 1.0 / (1.0 + jnp.exp(-v))


def step_kernel(
    ids, w_ref, x_hbm, film_hbm, cot_hbm, out, grad,
    W, R, BD, X, XT, H, GA, DA, ACC, FAR, TA, TB, RC, T, RY, A2, XB, PX, PP, ZB, ZR, RR, film, cot, cot_far,
    ls, hs, hr, cs, cr, es, er, s1, r1, s2, r2, s3, r3, s4, r4, s5, r5, m1, q1, m2, q2, m3, q3, m4, q4, m5, q5,
):
    lead, gy, gx, x, zh, core = place()
    zid = zh * 8 + lead
    west = x // 2
    block = gy % 2
    pair = gy - block
    sent = []

    def finish():
        for wait in sent:
            wait()

    x_in = pltpu.make_async_copy(x_hbm, X.at[0, 1], ls.at[0])
    film_in = pltpu.make_async_copy(film_hbm, film, ls.at[1])
    cot_in = pltpu.make_async_copy(cot_hbm, cot, ls.at[2])
    x_in.start()
    film_in.start()
    cot_in.start()
    R[zh, lead] = w_ref[...]
    x_in.wait()
    greet()

    far_first = (8, 7, 9, 6, 10, 5, 11, 4, 12, 3, 13, 2, 14, 1, 15)

    def needed(l, y):
        number = 2 * l + y // 2
        inside = ((number >= 1) & (number <= 3)) | ((number >= 7) & (number <= 8)) | ((number >= 12) & (number <= 14))
        return (y % 2 == 0) | inside

    def spread(k, both):
        own = R.at[zh, lead] if both else R.at[zh, lead, 0]
        return remote(own, own, s1.at[k], r1.at[k], **ring(k))

    def spread_in(k, both):
        z = (zid + 16 - k) % 16
        own = R.at[z // 8, z % 8] if both else R.at[z // 8, z % 8, 0]
        return remote(own, own, s1.at[k], r1.at[k], **ring(k))

    def each_spread(act):
        for both in (True, False):

            @pl.when(needed(lead, pair + 1) if both else jnp.logical_not(needed(lead, pair + 1)))
            def _():
                for k in far_first:
                    act(spread(k, both))

    def halo(col, up):
        return remote(
            X.at[col, 1], X.at[col, 0 if up else 2], hs.at[col, int(up)], hr.at[col, int(up)],
            gy=(gy + (1 if up else 3)) % 4,
        )

    def across(part):
        rows = pl.ds(256 * part, 256)
        return remote(X.at[0, 1, rows], X.at[1, 1, rows], hs.at[2, part], hr.at[2, part], gx=(gx + 8) % 16)

    def corner(part, up):
        rows = pl.ds(256 * part, 256)
        return remote(
            X.at[1, 1, rows], X.at[1, 0 if up else 2, rows], hs.at[1 + 2 * part, int(up)], hr.at[1 + 2 * part, int(up)],
            gy=(gy + (1 if up else 3)) % 4,
        )

    has = {True: gy < 3, False: gy > 0}
    gets = {True: gy > 0, False: gy < 3}
    for part in range(2):
        across(part).start()
        sent.append(across(part).wait_send)

    def halo_out():
        for up in (True, False):

            @pl.when(has[up])
            def _():
                halo(0, up).start()

    def corner_out(part):
        across(part).wait_recv()
        for up in (True, False):

            @pl.when(has[up])
            def _():
                corner(part, up).start()

    @sent.append
    def _():
        for up in (True, False):

            @pl.when(has[up])
            def _():
                halo(0, up).wait_send()
                corner(0, up).wait_send()
                corner(1, up).wait_send()

    def halo_in(col):
        for up in (True, False):

            @pl.when(gets[up])
            def _():
                if col == 0:
                    halo(0, up).wait_recv()
                else:
                    corner(0, up).wait_recv()
                    corner(1, up).wait_recv()

            @pl.when(jnp.logical_not(gets[up]))
            def _():
                X[col, 0 if up else 2] = jnp.zeros((512, 256), BF16)

    halo_out()
    each_spread(lambda copy: copy.start())
    sent.append(lambda: each_spread(lambda copy: copy.wait_send()))
    corner_out(0)
    XT[0, 1] = X[0, 1].T
    for k in far_first[::-1]:
        z = (zid + 16 - k) % 16
        for both in (True, False):

            @pl.when(needed(z % 8, pair + 1) if both else jnp.logical_not(needed(z % 8, pair + 1)))
            def _():
                spread_in(k, both).wait_recv()

    def gather(k):
        y, xx = (block + k // 8) % 2, (x + (k // 2) % 4) % 4
        return remote(
            R.at[:, pl.ds(2 * xx, 2), y], BD.at[block, x, core], s2.at[k], r2.at[block, x, core],
            gy=pair + y, gx=xx * 4 + zh * 2 + (core + k) % 2,
        )

    def gather_in(k):
        y, xx, c = (block + k // 8) % 2, (x + (k // 2) % 4) % 4, (core + k) % 2
        return remote(R.at[:, pl.ds(2 * x, 2), 0], BD.at[y, xx, c], s2.at[k], r2.at[y, xx, c], gy=gy, gx=gx)

    for k in range(1, 16):
        gather(k).start()
        sent.append(gather(k).wait_send)
    BD[block, x, core] = R[:, pl.ds(2 * x, 2), block]
    row = lax.broadcasted_iota(jnp.int32, (144, 512), 0) * 2 + core
    column = lax.broadcasted_iota(jnp.int32, (144, 512), 1)
    owner = (row * 57) >> 9
    place_of = ((owner >> 2) * 2 + (owner & 1)) * 2 + ((owner >> 1) & 1)
    pick = (column == place_of * 16 + (row - owner * 9)).astype(F32).astype(BF16)
    corner_out(1)
    cot_in.wait()
    cot_out = remote(cot, cot_far, es, er, gy=(gy + 2) % 4)
    cot_out.start()
    sent.append(cot_out.wait_send)
    for k in range(1, 16):
        gather_in(k).wait_recv()

    def piece(l, y, sems, slot, **where):
        part = W.at[core, y % 2, group(l, y)]
        return remote(part, part, sems[0].at[slot], sems[1].at[slot], **where)

    def start_if(l, y, copy):
        @pl.when(needed(l, y))
        def _():
            copy.start()

        @sent.append
        def _():
            @pl.when(needed(l, y))
            def _():
                copy.wait_send()

    def wait_if(l, y, copy):
        @pl.when(needed(l, y))
        def _():
            copy.wait_recv()

    order = (1, 3, 2)

    def to_y(k):
        return {"gy": (gy + k) % 4}

    def to_x(k):
        return {"gx": (gx + 4 * k) % 16}

    for j in range(2):
        W[core, block, group(2 * x + j, gy), :] = jnp.dot(
            pick, BD[:, :, :, :, j].reshape(512, 128), preferred_element_type=F32
        ).astype(BF16)
        for k in order:
            l = 2 * x + j
            start_if(l, gy, piece(l, gy, (s3, r3), (j, k - 1), **(to_x(k) if j else to_y(k))))
        for k in order:
            l = 2 * x + j
            start_if(l, gy, piece(l, gy, (s4, r4), (j, 0, k - 1), **(to_y(k) if j else to_x(k))))
    XT[1, 1] = X[1, 1].T
    for n in order:
        for j in range(2):
            l, y = (2 * ((x + 4 - n) % 4) + 1, gy) if j else (2 * x, (gy + 4 - n) % 4)
            wait_if(l, y, piece(l, y, (s3, r3), (j, n - 1), gx=gx))
            for k in order:
                start_if(l, y, piece(l, y, (s4, r4), (j, n, k - 1), **(to_y(k) if j else to_x(k))))
    for col in range(2):
        halo_in(col)
        for a in (0, 2):
            XT[col, a] = X[col, a].T
    for tap in range(3):
        at = pl.ds(pl.multiple_of((3 * tap + 2 * west) * 256, 256), 256)
        TA[at, :] = jnp.zeros((256, 128), F32)
        RC[at, :] = jnp.zeros((256, 128), F32)
    for n in (0,) + order:
        for k in order:
            for j in range(2):
                if j:
                    l, y = 2 * ((x + 4 - n) % 4) + 1, (gy + 4 - k) % 4
                else:
                    l, y = 2 * ((x + 4 - k) % 4), (gy + 4 - n) % 4
                wait_if(l, y, piece(l, y, (s4, r4), (j, n, k - 1), gx=gx))

    def to_mate(part, start):
        h = core if start else 1 - core
        rows = pl.ds(0, 2304) if part == 0 else pl.ds(256 + 768 * (part - 1), 256)
        view = W.at[h, min(part, 1), rows]
        return remote(view, view, s5.at[part], r5.at[part], gx=gx + 1 - 2 * core)

    for part in range(4):
        to_mate(part, True).start()
        sent.append(to_mate(part, True).wait_send)
    film_in.wait()
    to_mate(0, False).wait_recv()

    row = film[ids[0]]
    mult_a, shift_a, mult_b, shift_b = 1.0 + row[0:1], row[1:2], 1.0 + row[2:3], row[3:4]

    def half(h, block, tap):
        return W[h, block, pl.ds(pl.multiple_of(tap * 256, 256), 256), :]

    def weight(block, tap):
        return jnp.concatenate([half(0, block, tap), half(1, block, tap)], axis=1)

    taps = [(0, 1, 1 + 3), (0, 0, 1), (0, 2, 7)] + [(1, a, 3 * a + 2 - 2 * west) for a in (1, 0, 2)]

    def rows_of(m):
        return pl.ds(pl.multiple_of(m * ROWS, ROWS), ROWS)

    def send_hidden(m):
        return remote(H.at[0, rows_of(m)], H.at[1, rows_of(m)], cs.at[m], cr.at[m], gy=(gy + 2) % 4)

    @pl.loop(0, CHUNKS)
    def _(m):
        r = rows_of(m)
        pre = jnp.zeros((ROWS, 256), F32)
        for col, a, tap in taps:
            pre = pre + jnp.dot(X[col, a, r, :], weight(0, tap), preferred_element_type=F32)
        pre = pre * mult_a + shift_a
        sig = sigmoid(pre)
        H[0, r, :] = (X[0, 1, r, :].astype(F32) + pre * sig).astype(BF16)
        DA[r, :] = mult_a * sig * (1.0 + pre * (1.0 - sig))
        send_hidden(m).start()

    @sent.append
    def _():
        @pl.loop(0, CHUNKS)
        def _(m):
            send_hidden(m).wait_send()

    for part in range(1, 4):
        to_mate(part, False).wait_recv()
    south = gy // 2

    def back_dot(value, tap):
        turned = (((1,), (1,)), ((), ()))
        return lax.dot_general(
            value[:, :128], half(0, 1, tap), turned, preferred_element_type=F32
        ) + lax.dot_general(value[:, 128:], half(1, 1, tap), turned, preferred_element_type=F32)

    @pl.loop(0, CHUNKS)
    def _(m):
        r = rows_of(m)
        ACC[r, :] = jnp.dot(H[0, r, :], weight(1, 4), preferred_element_type=F32)
        FAR[r, :] = jnp.dot(H[0, r, :], weight(1, 1 + 6 * south), preferred_element_type=F32)

    cot_out.wait_recv()

    @pl.loop(0, CHUNKS)
    def _(m):
        r = rows_of(m)
        send_hidden(m).wait_recv()
        other = H[1, r, :]
        pre = ACC[r, :] + jnp.dot(other, weight(1, 7 - 6 * south), preferred_element_type=F32)
        pre = pre * mult_b + shift_b
        sig = sigmoid(pre)
        out[r, :] = (H[0, r, :].astype(F32) + pre * sig).astype(BF16)
        up = cot[r, :].astype(F32)
        near_grad = (up * mult_b * sig * (1.0 + pre * (1.0 - sig))).astype(BF16)
        pre = jnp.dot(other, weight(1, 4), preferred_element_type=F32) + FAR[r, :]
        pre = pre * mult_b + shift_b
        sig = sigmoid(pre)
        far_grad = (cot_far[r, :].astype(F32) * mult_b * sig * (1.0 + pre * (1.0 - sig))).astype(BF16)
        back = up + back_dot(near_grad, 4) + back_dot(far_grad, 1 + 6 * south)
        value = back * DA[r, :]
        left, right = value[:, :128], value[:, 128:]
        GA[r, :] = jnp.concatenate(
            [jnp.where(core == 0, left, right), jnp.where(core == 0, right, left)], axis=1
        ).astype(BF16)

    scale = 1.0 / 512.0

    def mate(tap):
        at = pl.ds(pl.multiple_of(tap * 256, 256), 256)
        return remote(TB.at[at], RC.at[at], m1.at[tap], q1.at[tap], gx=gx + 1 - 2 * core)

    for col, a, tap in taps:
        at = pl.ds(pl.multiple_of(tap * 256, 256), 256)
        term = jnp.dot(XT[col, a], GA[...], preferred_element_type=F32) * scale
        TB[at, :] = term[:, 128:]
        mate(tap).start()
        sent.append(mate(tap).wait_send)
        TA[at, :] = term[:, :128]
    for col, a, tap in taps:
        mate(tap).wait_recv()

    def rows72(l, y):
        return pl.ds(pl.multiple_of((l * 4 + y) * 72, 8), 72)

    def empty(l, y):
        number = 4 * l + y
        first = ((number >= 0) & (number <= 2)) | ((number >= 11) & (number <= 13)) | ((number >= 22) & (number <= 23))
        last = ((number >= 8) & (number <= 9)) | ((number >= 18) & (number <= 20)) | (number >= 29)
        return ((west == 0) & first) | ((west == 1) & last)

    def sum_y(k, l):
        return remote(T.at[k - 1, l], RY.at[k - 1, l], m2.at[k - 1, l], q2.at[k - 1, l], gy=(gy + k) % 4)

    for k in order:

        @pl.loop(0, 8)
        def _(l):
            at = rows72(l, (gy + k) % 4)

            @pl.when(jnp.logical_not(empty(l, (gy + k) % 4)))
            def _():
                T[k - 1, l] = (TA[at, :] + RC[at, :]).astype(BF16)
                sum_y(k, l).start()

    @sent.append
    def _():
        for k in order:

            @pl.loop(0, 8)
            def _(l):
                @pl.when(jnp.logical_not(empty(l, (gy + k) % 4)))
                def _():
                    sum_y(k, l).wait_send()

    @pl.loop(0, 8)
    def _(l):
        at = rows72(l, gy)
        A2[l] = TA[at, :] + RC[at, :]

    for k in order:

        @pl.loop(0, 8)
        def _(l):
            @pl.when(jnp.logical_not(empty(l, gy)))
            def _():
                sum_y(k, l).wait_recv()
                A2[l] += RY[k - 1, l].astype(F32)

    def sum_x(k):
        return remote(XB.at[k - 1], PX.at[k - 1], m3.at[k - 1], q3.at[k - 1], gx=(gx + 4 * k) % 16)

    def window(xx):
        return A2[:, pl.ds(pl.multiple_of(xx * 16, 16), 24), :]

    for k in order:
        XB[k - 1] = window((x + k) % 4).astype(BF16)
        sum_x(k).start()
        sent.append(sum_x(k).wait_send)
    PP[...] = window(x)
    for k in order:
        sum_x(k).wait_recv()
    P = PP[...] + PX[0].astype(F32) + PX[1].astype(F32) + PX[2].astype(F32)
    PP[...] = P
    ZB[0] = P[:, 0:16].astype(BF16)
    ZB[1] = P[:, 8:24].astype(BF16)

    def sum_z(k):
        z = (zid + k) % 16
        return remote(ZB.at[z // 8, z % 8], ZR.at[k], m4.at[k], q4.at[k], **ring(k))

    for k in far_first:
        sum_z(k).start()
        sent.append(sum_z(k).wait_send)
    total = PP[lead, pl.ds(pl.multiple_of(zh * 8, 8), 16), :]
    for k in far_first[::-1]:
        sum_z(k).wait_recv()
        total = total + ZR[k].astype(F32)
    RR[core] = total
    swap = remote(RR.at[core], RR.at[core], m5, q5, gx=gx + 1 - 2 * core)
    swap_in = remote(RR.at[1 - core], RR.at[1 - core], m5, q5, gx=gx + 1 - 2 * core)
    swap.start()
    sent.append(swap.wait_send)
    swap_in.wait_recv()
    for j in range(9):
        grad[j : j + 1, :] = RR[(j + core) % 2, pl.ds(2 * x + zh + (9 * core + j) // 2, 1), :]
    finish()


def shards(inputs, lead_ids, film, flat_weights, cotangent):
    padded = jnp.pad(flat_weights.reshape(2, 9, 128), ((0, 0), (0, 7), (0, 0)))
    vmem = pl.BlockSpec(memory_space=pltpu.VMEM)
    hbm = pl.BlockSpec(memory_space=pltpu.HBM)
    outputs, total = pl.pallas_call(
        step_kernel,
        out_shape=(jax.ShapeDtypeStruct((512, 256), BF16), jax.ShapeDtypeStruct((9, 128), F32)),
        in_specs=[pl.BlockSpec(memory_space=pltpu.SMEM), vmem, hbm, hbm, hbm],
        out_specs=(vmem, vmem),
        scratch_shapes=[
            pltpu.VMEM((2, 2, 2304, 128), BF16),
            pltpu.VMEM((2, 8, 2, 16, 128), BF16),
            pltpu.VMEM((2, 4, 2, 2, 2, 16, 128), BF16),
            pltpu.VMEM((2, 3, 512, 256), BF16),
            pltpu.VMEM((2, 3, 256, 512), BF16),
            pltpu.VMEM((2, 512, 256), BF16),
            pltpu.VMEM((512, 256), BF16),
            pltpu.VMEM((512, 256), F32),
            pltpu.VMEM((512, 256), F32),
            pltpu.VMEM((512, 256), F32),
            pltpu.VMEM((2304, 128), F32),
            pltpu.VMEM((2304, 128), F32),
            pltpu.VMEM((2304, 128), F32),
            pltpu.VMEM((3, 8, 72, 128), BF16),
            pltpu.VMEM((3, 8, 72, 128), BF16),
            pltpu.VMEM((8, 72, 128), F32),
            pltpu.VMEM((3, 8, 24, 128), BF16),
            pltpu.VMEM((3, 8, 24, 128), BF16),
            pltpu.VMEM((8, 24, 128), F32),
            pltpu.VMEM((2, 8, 16, 128), BF16),
            pltpu.VMEM((16, 16, 128), BF16),
            pltpu.VMEM((2, 16, 128), F32),
            pltpu.VMEM((360, 4, 256), F32),
            pltpu.VMEM((512, 256), BF16),
            pltpu.VMEM((512, 256), BF16),
            DMA((3,)),
            DMA((4, 2)), DMA((4, 2)),
            DMA((CHUNKS,)), DMA((CHUNKS,)),
            DMA(()), DMA(()),
            DMA((16,)), DMA((16,)),
            DMA((16,)), DMA((2, 4, 2)),
            DMA((2, 3)), DMA((2, 3)),
            DMA((2, 4, 3)), DMA((2, 4, 3)),
            DMA((4,)), DMA((4,)),
            DMA((9,)), DMA((9,)),
            DMA((3, 8)), DMA((3, 8)),
            DMA((3,)), DMA((3,)),
            DMA((16,)), DMA((16,)),
            DMA(()), DMA(()),
        ],
        compiler_params=pltpu.CompilerParams(
            collective_id=0, has_side_effects=True, vmem_limit_bytes=50 << 20
        ),
    )(lead_ids, padded, inputs.reshape(512, 256), film, cotangent.reshape(512, 256))
    return (outputs.reshape(inputs.shape), total.reshape(-1))


def solution(mesh):
    return jax.shard_map(
        shards,
        mesh=mesh,
        in_specs=(
            P("lead", "gy", "gx", None),
            P("lead"),
            P(),
            P(None, ("lead", "gy", "gx")),
            P("lead", "gy", "gx", None),
        ),
        out_specs=(P("lead", "gy", "gx", None), P(("lead", "gy", "gx"))),
        check_vma=False,
    )
```

```python
import jax
import jax.numpy as jnp
from jax import lax
from jax.experimental import pallas as pl
from jax.experimental.pallas import tpu as pltpu
from jax.sharding import PartitionSpec as P

MESH = pl.DeviceIdType.MESH
DMA = pltpu.SemaphoreType.DMA
F32, BF16 = jnp.float32, jnp.bfloat16


def place():
    lead, gy, gx = lax.axis_index("lead"), lax.axis_index("gy"), lax.axis_index("gx")
    return lead, gy, gx, gx // 4, (gx // 2) % 2, gx % 2


def remote(src, dst, send_sem, recv_sem, **where):
    return pltpu.make_async_remote_copy(
        src_ref=src, dst_ref=dst, send_sem=send_sem, recv_sem=recv_sem, device_id=where, device_id_type=MESH
    )


def greet():
    lead, gy, gx, x, zh, core = place()
    barrier = pltpu.get_barrier_semaphore()
    first = gy - gy % 2

    def hello(**where):
        pl.semaphore_signal(barrier, inc=1, device_id=where, device_id_type=MESH)

    for k in range(1, 16):
        hello(**ring(k))
    hello(gy=(gy + 2) % 4)
    hello(gy=3 - gy)
    for k in range(1, 16):
        hello(gy=first + (gy % 2 + k // 8) % 2, gx=(x + (k // 2) % 4) % 4 * 4 + zh * 2 + (core + k) % 2)
    pl.semaphore_wait(barrier, 32)


def ring(k):
    lead, gy, gx, x, zh, core = place()
    z = (zh * 8 + lead + k) % 16
    return {"lead": z % 8, "gx": x * 4 + (z // 8) * 2 + core}


ROWS = 128
CHUNKS = 4


def group(lead, gy):
    return pl.ds(pl.multiple_of((lead * 2 + gy // 2) * 144, 16), 144)


def quarter(x):
    return pl.ds(pl.multiple_of(x * 576, 64), 576)


def sigmoid(v):
    return 1.0 / (1.0 + jnp.exp(-v))


def step_kernel(
    ids, w_ref, x_hbm, film_hbm, cot_hbm, out, grad,
    W, R, BD, X, XT, H, GA, DA, ACC, FAR, TA, TB, RC, T, RY, A2, XB, PX, PP, ZB, ZR, RR, film, cot, cot_far,
    ls, hs, hr, cs, cr, es, er, s1, r1, s2, r2, s3, r3, s4, r4, s5, r5, m1, q1, m2, q2, m3, q3, m4, q4, m5, q5,
):
    lead, gy, gx, x, zh, core = place()
    zid = zh * 8 + lead
    west = x // 2
    block = gy % 2
    pair = gy - block
    sent = []

    def finish():
        for wait in sent:
            wait()

    x_in = pltpu.make_async_copy(x_hbm, X.at[0, 1], ls.at[0])
    film_in = pltpu.make_async_copy(film_hbm, film, ls.at[1])
    cot_in = pltpu.make_async_copy(cot_hbm, cot, ls.at[2])
    x_in.start()
    film_in.start()
    cot_in.start()
    R[zh, lead] = w_ref[...]
    x_in.wait()
    greet()

    far_first = (8, 7, 9, 6, 10, 5, 11, 4, 12, 3, 13, 2, 14, 1, 15)

    def needed(l, y):
        number = 2 * l + y // 2
        inside = ((number >= 1) & (number <= 3)) | ((number >= 7) & (number <= 8)) | ((number >= 12) & (number <= 14))
        return (y % 2 == 0) | inside

    def spread(k, both):
        own = R.at[zh, lead] if both else R.at[zh, lead, 0]
        return remote(own, own, s1.at[k], r1.at[k], **ring(k))

    def spread_in(k, both):
        z = (zid + 16 - k) % 16
        own = R.at[z // 8, z % 8] if both else R.at[z // 8, z % 8, 0]
        return remote(own, own, s1.at[k], r1.at[k], **ring(k))

    def each_spread(act):
        for both in (True, False):

            @pl.when(needed(lead, pair + 1) if both else jnp.logical_not(needed(lead, pair + 1)))
            def _():
                for k in far_first:
                    act(spread(k, both))

    def halo(col, up):
        return remote(
            X.at[col, 1], X.at[col, 0 if up else 2], hs.at[col, int(up)], hr.at[col, int(up)],
            gy=(gy + (1 if up else 3)) % 4,
        )

    def across(part):
        rows = pl.ds(256 * part, 256)
        return remote(X.at[0, 1, rows], X.at[1, 1, rows], hs.at[2, part], hr.at[2, part], gx=(gx + 8) % 16)

    def corner(part, up):
        rows = pl.ds(256 * part, 256)
        return remote(
            X.at[1, 1, rows], X.at[1, 0 if up else 2, rows], hs.at[1 + 2 * part, int(up)], hr.at[1 + 2 * part, int(up)],
            gy=(gy + (1 if up else 3)) % 4,
        )

    has = {True: gy < 3, False: gy > 0}
    gets = {True: gy > 0, False: gy < 3}
    for part in range(2):
        across(part).start()
        sent.append(across(part).wait_send)

    def halo_out():
        for up in (True, False):

            @pl.when(has[up])
            def _():
                halo(0, up).start()

    def corner_out(part):
        across(part).wait_recv()
        for up in (True, False):

            @pl.when(has[up])
            def _():
                corner(part, up).start()

    @sent.append
    def _():
        for up in (True, False):

            @pl.when(has[up])
            def _():
                halo(0, up).wait_send()
                corner(0, up).wait_send()
                corner(1, up).wait_send()

    def halo_in(col):
        for up in (True, False):

            @pl.when(gets[up])
            def _():
                if col == 0:
                    halo(0, up).wait_recv()
                else:
                    corner(0, up).wait_recv()
                    corner(1, up).wait_recv()

            @pl.when(jnp.logical_not(gets[up]))
            def _():
                X[col, 0 if up else 2] = jnp.zeros((512, 256), BF16)

    halo_out()
    each_spread(lambda copy: copy.start())
    sent.append(lambda: each_spread(lambda copy: copy.wait_send()))
    corner_out(0)
    XT[0, 1] = X[0, 1].T
    for k in far_first[::-1]:
        z = (zid + 16 - k) % 16
        for both in (True, False):

            @pl.when(needed(z % 8, pair + 1) if both else jnp.logical_not(needed(z % 8, pair + 1)))
            def _():
                spread_in(k, both).wait_recv()

    def gather(k):
        y, xx = (block + k // 8) % 2, (x + (k // 2) % 4) % 4
        return remote(
            R.at[:, pl.ds(2 * xx, 2), y], BD.at[block, x, core], s2.at[k], r2.at[block, x, core],
            gy=pair + y, gx=xx * 4 + zh * 2 + (core + k) % 2,
        )

    def gather_in(k):
        y, xx, c = (block + k // 8) % 2, (x + (k // 2) % 4) % 4, (core + k) % 2
        return remote(R.at[:, pl.ds(2 * x, 2), 0], BD.at[y, xx, c], s2.at[k], r2.at[y, xx, c], gy=gy, gx=gx)

    for k in range(1, 16):
        gather(k).start()
        sent.append(gather(k).wait_send)
    BD[block, x, core] = R[:, pl.ds(2 * x, 2), block]
    row = lax.broadcasted_iota(jnp.int32, (144, 512), 0) * 2 + core
    column = lax.broadcasted_iota(jnp.int32, (144, 512), 1)
    owner = (row * 57) >> 9
    place_of = ((owner >> 2) * 2 + (owner & 1)) * 2 + ((owner >> 1) & 1)
    pick = (column == place_of * 16 + (row - owner * 9)).astype(F32).astype(BF16)
    corner_out(1)
    cot_in.wait()
    cot_out = remote(cot, cot_far, es, er, gy=(gy + 2) % 4)
    cot_out.start()
    sent.append(cot_out.wait_send)
    halo_in(0)
    XT[0, 0] = X[0, 0].T
    XT[0, 2] = X[0, 2].T
    for k in range(1, 16):
        gather_in(k).wait_recv()

    def piece(l, y, sems, slot, **where):
        part = W.at[core, y % 2, group(l, y)]
        return remote(part, part, sems[0].at[slot], sems[1].at[slot], **where)

    def start_if(l, y, copy):
        @pl.when(needed(l, y))
        def _():
            copy.start()

        @sent.append
        def _():
            @pl.when(needed(l, y))
            def _():
                copy.wait_send()

    def wait_if(l, y, copy):
        @pl.when(needed(l, y))
        def _():
            copy.wait_recv()

    order = (1, 3, 2)

    def to_y(k):
        return {"gy": (gy + k) % 4}

    def to_x(k):
        return {"gx": (gx + 4 * k) % 16}

    for j in range(2):
        W[core, block, group(2 * x + j, gy), :] = jnp.dot(
            pick, BD[:, :, :, :, j].reshape(512, 128), preferred_element_type=F32
        ).astype(BF16)
        for k in order:
            l = 2 * x + j
            start_if(l, gy, piece(l, gy, (s3, r3), (j, k - 1), **(to_x(k) if j else to_y(k))))
        for k in order:
            l = 2 * x + j
            start_if(l, gy, piece(l, gy, (s4, r4), (j, 0, k - 1), **(to_y(k) if j else to_x(k))))
    for n in order:
        for j in range(2):
            l, y = (2 * ((x + 4 - n) % 4) + 1, gy) if j else (2 * x, (gy + 4 - n) % 4)
            wait_if(l, y, piece(l, y, (s3, r3), (j, n - 1), gx=gx))
            for k in order:
                start_if(l, y, piece(l, y, (s4, r4), (j, n, k - 1), **(to_y(k) if j else to_x(k))))
    for tap in range(3):
        at = pl.ds(pl.multiple_of((3 * tap + 2 * west) * 256, 256), 256)
        TA[at, :] = jnp.zeros((256, 128), F32)
        RC[at, :] = jnp.zeros((256, 128), F32)
    for n in (0,) + order:
        for k in order:
            for j in range(2):
                if j:
                    l, y = 2 * ((x + 4 - n) % 4) + 1, (gy + 4 - k) % 4
                else:
                    l, y = 2 * ((x + 4 - k) % 4), (gy + 4 - n) % 4
                wait_if(l, y, piece(l, y, (s4, r4), (j, n, k - 1), gx=gx))

    def to_mate(part, start):
        h = core if start else 1 - core
        rows = pl.ds(0, 2304) if part == 0 else pl.ds(256 + 768 * (part - 1), 256)
        view = W.at[h, min(part, 1), rows]
        return remote(view, view, s5.at[part], r5.at[part], gx=gx + 1 - 2 * core)

    for part in range(4):
        to_mate(part, True).start()
        sent.append(to_mate(part, True).wait_send)
    film_in.wait()
    halo_in(1)
    to_mate(0, False).wait_recv()

    row = film[ids[0]]
    mult_a, shift_a, mult_b, shift_b = 1.0 + row[0:1], row[1:2], 1.0 + row[2:3], row[3:4]

    def half(h, block, tap):
        return W[h, block, pl.ds(pl.multiple_of(tap * 256, 256), 256), :]

    def weight(block, tap):
        return jnp.concatenate([half(0, block, tap), half(1, block, tap)], axis=1)

    taps = [(0, 1, 1 + 3), (0, 0, 1), (0, 2, 7)] + [(1, a, 3 * a + 2 - 2 * west) for a in (1, 0, 2)]

    def rows_of(m):
        return pl.ds(pl.multiple_of(m * ROWS, ROWS), ROWS)

    def send_hidden(m):
        return remote(H.at[0, rows_of(m)], H.at[1, rows_of(m)], cs.at[m], cr.at[m], gy=(gy + 2) % 4)

    @pl.loop(0, CHUNKS)
    def _(m):
        r = rows_of(m)
        pre = jnp.zeros((ROWS, 256), F32)
        for col, a, tap in taps:
            pre = pre + jnp.dot(X[col, a, r, :], weight(0, tap), preferred_element_type=F32)
        pre = pre * mult_a + shift_a
        sig = sigmoid(pre)
        H[0, r, :] = (X[0, 1, r, :].astype(F32) + pre * sig).astype(BF16)
        DA[r, :] = mult_a * sig * (1.0 + pre * (1.0 - sig))
        send_hidden(m).start()

    @sent.append
    def _():
        @pl.loop(0, CHUNKS)
        def _(m):
            send_hidden(m).wait_send()

    for part in range(1, 4):
        to_mate(part, False).wait_recv()
    south = gy // 2

    def back_dot(value, tap):
        turned = (((1,), (1,)), ((), ()))
        return lax.dot_general(
            value[:, :128], half(0, 1, tap), turned, preferred_element_type=F32
        ) + lax.dot_general(value[:, 128:], half(1, 1, tap), turned, preferred_element_type=F32)

    @pl.loop(0, CHUNKS)
    def _(m):
        r = rows_of(m)
        ACC[r, :] = jnp.dot(H[0, r, :], weight(1, 4), preferred_element_type=F32)
        FAR[r, :] = jnp.dot(H[0, r, :], weight(1, 1 + 6 * south), preferred_element_type=F32)

    for a in range(3):
        XT[1, a] = X[1, a].T
    cot_out.wait_recv()

    @pl.loop(0, CHUNKS)
    def _(m):
        r = rows_of(m)
        send_hidden(m).wait_recv()
        other = H[1, r, :]
        pre = ACC[r, :] + jnp.dot(other, weight(1, 7 - 6 * south), preferred_element_type=F32)
        pre = pre * mult_b + shift_b
        sig = sigmoid(pre)
        out[r, :] = (H[0, r, :].astype(F32) + pre * sig).astype(BF16)
        up = cot[r, :].astype(F32)
        near_grad = (up * mult_b * sig * (1.0 + pre * (1.0 - sig))).astype(BF16)
        pre = jnp.dot(other, weight(1, 4), preferred_element_type=F32) + FAR[r, :]
        pre = pre * mult_b + shift_b
        sig = sigmoid(pre)
        far_grad = (cot_far[r, :].astype(F32) * mult_b * sig * (1.0 + pre * (1.0 - sig))).astype(BF16)
        back = up + back_dot(near_grad, 4) + back_dot(far_grad, 1 + 6 * south)
        value = back * DA[r, :]
        left, right = value[:, :128], value[:, 128:]
        GA[r, :] = jnp.concatenate(
            [jnp.where(core == 0, left, right), jnp.where(core == 0, right, left)], axis=1
        ).astype(BF16)

    scale = 1.0 / 512.0

    def mate(tap):
        at = pl.ds(pl.multiple_of(tap * 256, 256), 256)
        return remote(TB.at[at], RC.at[at], m1.at[tap], q1.at[tap], gx=gx + 1 - 2 * core)

    def rows72(l, y):
        return pl.ds(pl.multiple_of((l * 4 + y) * 72, 8), 72)

    def empty(l, y):
        number = 4 * l + y
        first = ((number >= 0) & (number <= 2)) | ((number >= 11) & (number <= 13)) | ((number >= 22) & (number <= 23))
        last = ((number >= 8) & (number <= 9)) | ((number >= 18) & (number <= 20)) | (number >= 29)
        return ((west == 0) & first) | ((west == 1) & last)

    def sum_y(k, l):
        return remote(T.at[k - 1, l], RY.at[k - 1, l], m2.at[k - 1, l], q2.at[k - 1, l], gy=(gy + k) % 4)

    def send_rows(a, first, last):
        for col in range(2):
            mate(row_taps[a][col][2]).wait_recv()

        @pl.loop(first, last)
        def _(l):
            for k in order:
                at = rows72(l, (gy + k) % 4)

                @pl.when(jnp.logical_not(empty(l, (gy + k) % 4)))
                def _():
                    T[k - 1, l] = (TA[at, :] + RC[at, :]).astype(BF16)
                    sum_y(k, l).start()

    row_taps = [[(0, a, 3 * a + 1), (1, a, 3 * a + 2 - 2 * west)] for a in range(3)]
    parts = ((0, 2), (2, 5), (5, 8))
    for a in range(3):
        for col, _, tap in row_taps[a]:
            at = pl.ds(pl.multiple_of(tap * 256, 256), 256)
            term = jnp.dot(XT[col, a], GA[...], preferred_element_type=F32) * scale
            TB[at, :] = term[:, 128:]
            mate(tap).start()
            sent.append(mate(tap).wait_send)
            TA[at, :] = term[:, :128]
        if a:
            send_rows(a - 1, *parts[a - 1])
    send_rows(2, *parts[2])

    @sent.append
    def _():
        for k in order:

            @pl.loop(0, 8)
            def _(l):
                @pl.when(jnp.logical_not(empty(l, (gy + k) % 4)))
                def _():
                    sum_y(k, l).wait_send()

    @pl.loop(0, 8)
    def _(l):
        at = rows72(l, gy)
        A2[l] = TA[at, :] + RC[at, :]

    def sum_x(k, h):
        part = pl.ds(4 * h, 4)
        return remote(XB.at[k - 1, part], PX.at[k - 1, part], m3.at[k - 1, h], q3.at[k - 1, h], gx=(gx + 4 * k) % 16)

    def window(xx, h):
        return A2[4 * h : 4 * h + 4, pl.ds(pl.multiple_of(xx * 16, 16), 24), :]

    for h in range(2):
        for k in order:

            @pl.loop(4 * h, 4 * h + 4)
            def _(l):
                @pl.when(jnp.logical_not(empty(l, gy)))
                def _():
                    sum_y(k, l).wait_recv()
                    A2[l] += RY[k - 1, l].astype(F32)

        for k in order:
            XB[k - 1, 4 * h : 4 * h + 4] = window((x + k) % 4, h).astype(BF16)
            sum_x(k, h).start()
            sent.append(sum_x(k, h).wait_send)

    def sum_z(k):
        z = (zid + k) % 16
        return remote(ZB.at[z // 8, z % 8], ZR.at[k], m4.at[k], q4.at[k], **ring(k))

    for h in range(2):
        P = window(x, h)
        for k in order:
            sum_x(k, h).wait_recv()
            P = P + PX[k - 1, 4 * h : 4 * h + 4].astype(F32)
        PP[4 * h : 4 * h + 4] = P
        ZB[0, 4 * h : 4 * h + 4] = P[:, 0:16].astype(BF16)
        ZB[1, 4 * h : 4 * h + 4] = P[:, 8:24].astype(BF16)
        for k in far_first:

            @pl.when((zid + k) % 8 // 4 == h)
            def _():
                sum_z(k).start()

    for k in far_first:
        sent.append(sum_z(k).wait_send)
    total = PP[lead, pl.ds(pl.multiple_of(zh * 8, 8), 16), :]
    for k in far_first[::-1]:
        sum_z(k).wait_recv()
        total = total + ZR[k].astype(F32)
    RR[core] = total
    swap = remote(RR.at[core], RR.at[core], m5, q5, gx=gx + 1 - 2 * core)
    swap_in = remote(RR.at[1 - core], RR.at[1 - core], m5, q5, gx=gx + 1 - 2 * core)
    swap.start()
    sent.append(swap.wait_send)
    swap_in.wait_recv()
    for j in range(9):
        grad[j : j + 1, :] = RR[(j + core) % 2, pl.ds(2 * x + zh + (9 * core + j) // 2, 1), :]
    finish()


def shards(inputs, lead_ids, film, flat_weights, cotangent):
    padded = jnp.pad(flat_weights.reshape(2, 9, 128), ((0, 0), (0, 7), (0, 0)))
    vmem = pl.BlockSpec(memory_space=pltpu.VMEM)
    hbm = pl.BlockSpec(memory_space=pltpu.HBM)
    outputs, total = pl.pallas_call(
        step_kernel,
        out_shape=(jax.ShapeDtypeStruct((512, 256), BF16), jax.ShapeDtypeStruct((9, 128), F32)),
        in_specs=[pl.BlockSpec(memory_space=pltpu.SMEM), vmem, hbm, hbm, hbm],
        out_specs=(vmem, vmem),
        scratch_shapes=[
            pltpu.VMEM((2, 2, 2304, 128), BF16),
            pltpu.VMEM((2, 8, 2, 16, 128), BF16),
            pltpu.VMEM((2, 4, 2, 2, 2, 16, 128), BF16),
            pltpu.VMEM((2, 3, 512, 256), BF16),
            pltpu.VMEM((2, 3, 256, 512), BF16),
            pltpu.VMEM((2, 512, 256), BF16),
            pltpu.VMEM((512, 256), BF16),
            pltpu.VMEM((512, 256), F32),
            pltpu.VMEM((512, 256), F32),
            pltpu.VMEM((512, 256), F32),
            pltpu.VMEM((2304, 128), F32),
            pltpu.VMEM((2304, 128), F32),
            pltpu.VMEM((2304, 128), F32),
            pltpu.VMEM((3, 8, 72, 128), BF16),
            pltpu.VMEM((3, 8, 72, 128), BF16),
            pltpu.VMEM((8, 72, 128), F32),
            pltpu.VMEM((3, 8, 24, 128), BF16),
            pltpu.VMEM((3, 8, 24, 128), BF16),
            pltpu.VMEM((8, 24, 128), F32),
            pltpu.VMEM((2, 8, 16, 128), BF16),
            pltpu.VMEM((16, 16, 128), BF16),
            pltpu.VMEM((2, 16, 128), F32),
            pltpu.VMEM((360, 4, 256), F32),
            pltpu.VMEM((512, 256), BF16),
            pltpu.VMEM((512, 256), BF16),
            DMA((3,)),
            DMA((4, 2)), DMA((4, 2)),
            DMA((CHUNKS,)), DMA((CHUNKS,)),
            DMA(()), DMA(()),
            DMA((16,)), DMA((16,)),
            DMA((16,)), DMA((2, 4, 2)),
            DMA((2, 3)), DMA((2, 3)),
            DMA((2, 4, 3)), DMA((2, 4, 3)),
            DMA((4,)), DMA((4,)),
            DMA((9,)), DMA((9,)),
            DMA((3, 8)), DMA((3, 8)),
            DMA((3, 2)), DMA((3, 2)),
            DMA((16,)), DMA((16,)),
            DMA(()), DMA(()),
        ],
        compiler_params=pltpu.CompilerParams(
            collective_id=0, has_side_effects=True, vmem_limit_bytes=50 << 20
        ),
    )(lead_ids, padded, inputs.reshape(512, 256), film, cotangent.reshape(512, 256))
    return (outputs.reshape(inputs.shape), total.reshape(-1))


def solution(mesh):
    return jax.shard_map(
        shards,
        mesh=mesh,
        in_specs=(
            P("lead", "gy", "gx", None),
            P("lead"),
            P(),
            P(None, ("lead", "gy", "gx")),
            P("lead", "gy", "gx", None),
        ),
        out_specs=(P("lead", "gy", "gx", None), P(("lead", "gy", "gx"))),
        check_vma=False,
    )
```

```python
import jax
import jax.numpy as jnp
from jax import lax
from jax.experimental import pallas as pl
from jax.experimental.pallas import tpu as pltpu
from jax.sharding import PartitionSpec as P

MESH = pl.DeviceIdType.MESH
DMA = pltpu.SemaphoreType.DMA
F32, BF16 = jnp.float32, jnp.bfloat16


def place():
    lead, gy, gx = lax.axis_index("lead"), lax.axis_index("gy"), lax.axis_index("gx")
    return lead, gy, gx, gx // 4, (gx // 2) % 2, gx % 2


def remote(src, dst, send_sem, recv_sem, **where):
    return pltpu.make_async_remote_copy(
        src_ref=src, dst_ref=dst, send_sem=send_sem, recv_sem=recv_sem, device_id=where, device_id_type=MESH
    )


def greet():
    lead, gy, gx, x, zh, core = place()
    barrier = pltpu.get_barrier_semaphore()
    first = gy - gy % 2

    def hello(**where):
        pl.semaphore_signal(barrier, inc=1, device_id=where, device_id_type=MESH)

    for k in range(1, 16):
        hello(**ring(k))
    hello(gy=(gy + 2) % 4)
    hello(gy=3 - gy)
    for k in (1, 2, 4, 6, 8, 10, 12, 14):
        hello(gy=first + (gy % 2 + k // 8) % 2, gx=(x + (k // 2) % 4) % 4 * 4 + zh * 2 + (core + k) % 2)
    pl.semaphore_wait(barrier, 25)


def ring(k):
    lead, gy, gx, x, zh, core = place()
    z = (zh * 8 + lead + k) % 16
    return {"lead": z % 8, "gx": x * 4 + (z // 8) * 2 + core}


ROWS = 128
CHUNKS = 4


def group(lead, gy):
    return pl.ds(pl.multiple_of((lead * 2 + gy // 2) * 144, 16), 144)


def quarter(x):
    return pl.ds(pl.multiple_of(x * 576, 64), 576)


def sigmoid(v):
    return 1.0 / (1.0 + jnp.exp(-v))


def step_kernel(
    ids, w_ref, x_hbm, film_hbm, cot_hbm, out, grad,
    W, R, BD, X, XT, H, GA, DA, ACC, FAR, TA, TB, RC, T, RY, A2, XB, PX, PP, ZB, ZR, RR, film, cot, cot_far,
    ls, hs, hr, cs, cr, es, er, s1, r1, s2, r2, s6, r6, s3, r3, s4, r4, s5, r5, m1, q1, m2, q2, m3, q3, m4, q4, m5, q5,
):
    lead, gy, gx, x, zh, core = place()
    zid = zh * 8 + lead
    west = x // 2
    block = gy % 2
    pair = gy - block
    sent = []

    def finish():
        for wait in sent:
            wait()

    x_in = pltpu.make_async_copy(x_hbm, X.at[0, 1], ls.at[0])
    film_in = pltpu.make_async_copy(film_hbm, film, ls.at[1])
    cot_in = pltpu.make_async_copy(cot_hbm, cot, ls.at[2])
    x_in.start()
    film_in.start()
    cot_in.start()
    R[zh, lead] = w_ref[...]
    x_in.wait()
    greet()

    far_first = (8, 7, 9, 6, 10, 5, 11, 4, 12, 3, 13, 2, 14, 1, 15)

    def needed(l, y):
        number = 2 * l + y // 2
        inside = ((number >= 1) & (number <= 3)) | ((number >= 7) & (number <= 8)) | ((number >= 12) & (number <= 14))
        return (y % 2 == 0) | inside

    def spread(k, both):
        own = R.at[zh, lead] if both else R.at[zh, lead, 0]
        return remote(own, own, s1.at[k], r1.at[k], **ring(k))

    def spread_in(k, both):
        z = (zid + 16 - k) % 16
        own = R.at[z // 8, z % 8] if both else R.at[z // 8, z % 8, 0]
        return remote(own, own, s1.at[k], r1.at[k], **ring(k))

    def each_spread(act):
        for both in (True, False):

            @pl.when(needed(lead, pair + 1) if both else jnp.logical_not(needed(lead, pair + 1)))
            def _():
                for k in far_first:
                    act(spread(k, both))

    def halo(col, up):
        return remote(
            X.at[col, 1], X.at[col, 0 if up else 2], hs.at[col, int(up)], hr.at[col, int(up)],
            gy=(gy + (1 if up else 3)) % 4,
        )

    def across(part):
        rows = pl.ds(256 * part, 256)
        return remote(X.at[0, 1, rows], X.at[1, 1, rows], hs.at[2, part], hr.at[2, part], gx=(gx + 8) % 16)

    def corner(part, up):
        rows = pl.ds(256 * part, 256)
        return remote(
            X.at[1, 1, rows], X.at[1, 0 if up else 2, rows], hs.at[1 + 2 * part, int(up)], hr.at[1 + 2 * part, int(up)],
            gy=(gy + (1 if up else 3)) % 4,
        )

    has = {True: gy < 3, False: gy > 0}
    gets = {True: gy > 0, False: gy < 3}
    for part in range(2):
        across(part).start()
        sent.append(across(part).wait_send)

    def halo_out():
        for up in (True, False):

            @pl.when(has[up])
            def _():
                halo(0, up).start()

    def corner_out(part):
        across(part).wait_recv()
        for up in (True, False):

            @pl.when(has[up])
            def _():
                corner(part, up).start()

    @sent.append
    def _():
        for up in (True, False):

            @pl.when(has[up])
            def _():
                halo(0, up).wait_send()
                corner(0, up).wait_send()
                corner(1, up).wait_send()

    def halo_in(col):
        for up in (True, False):

            @pl.when(gets[up])
            def _():
                if col == 0:
                    halo(0, up).wait_recv()
                else:
                    corner(0, up).wait_recv()
                    corner(1, up).wait_recv()

            @pl.when(jnp.logical_not(gets[up]))
            def _():
                X[col, 0 if up else 2] = jnp.zeros((512, 256), BF16)

    halo_out()
    each_spread(lambda copy: copy.start())
    sent.append(lambda: each_spread(lambda copy: copy.wait_send()))
    corner_out(0)
    corner_out(1)
    cot_in.wait()
    cot_out = remote(cot, cot_far, es, er, gy=(gy + 2) % 4)
    cot_out.start()
    sent.append(cot_out.wait_send)
    XT[0, 1] = X[0, 1].T
    for k in far_first[::-1]:
        z = (zid + 16 - k) % 16
        for both in (True, False):

            @pl.when(needed(z % 8, pair + 1) if both else jnp.logical_not(needed(z % 8, pair + 1)))
            def _():
                spread_in(k, both).wait_recv()

    def gather(k):
        y, xx = (block + k // 4) % 2, (x + k) % 4
        return remote(
            R.at[:, pl.ds(2 * xx, 2), y], BD.at[core, block, x], s2.at[k], r2.at[block, x],
            gy=pair + y, gx=xx * 4 + zh * 2 + core,
        )

    def gather_in(k):
        y, xx = (block + k // 4) % 2, (x + k) % 4
        return remote(R.at[:, pl.ds(2 * x, 2), 0], BD.at[core, y, xx], s2.at[k], r2.at[y, xx], gy=gy, gx=gx)

    for k in range(1, 8):
        gather(k).start()
        sent.append(gather(k).wait_send)
    BD[core, block, x] = R[:, pl.ds(2 * x, 2), block]
    row = lax.broadcasted_iota(jnp.int32, (144, 512), 0) * 2 + core
    column = lax.broadcasted_iota(jnp.int32, (144, 512), 1)
    owner = (row * 57) >> 9
    place_of = (owner & 1) * 16 + (owner >> 2) * 2 + ((owner >> 1) & 1)
    pick = (column == place_of * 16 + (row - owner * 9)).astype(F32).astype(BF16)
    halo_in(0)
    XT[0, 0] = X[0, 0].T
    for k in range(1, 8):
        gather_in(k).wait_recv()
    swap_rows = remote(BD.at[core], BD.at[core], s6, r6, gx=gx + 1 - 2 * core)
    swap_rows.start()
    sent.append(swap_rows.wait_send)
    XT[0, 2] = X[0, 2].T
    remote(BD.at[1 - core], BD.at[1 - core], s6, r6, gx=gx + 1 - 2 * core).wait_recv()

    def piece(l, y, sems, slot, **where):
        part = W.at[core, y % 2, group(l, y)]
        return remote(part, part, sems[0].at[slot], sems[1].at[slot], **where)

    def start_if(l, y, copy):
        @pl.when(needed(l, y))
        def _():
            copy.start()

        @sent.append
        def _():
            @pl.when(needed(l, y))
            def _():
                copy.wait_send()

    def wait_if(l, y, copy):
        @pl.when(needed(l, y))
        def _():
            copy.wait_recv()

    order = (1, 3, 2)

    def to_y(k):
        return {"gy": (gy + k) % 4}

    def to_x(k):
        return {"gx": (gx + 4 * k) % 16}

    for j in range(2):
        W[core, block, group(2 * x + j, gy), :] = jnp.dot(
            pick, BD[:, :, :, :, j].reshape(512, 128), preferred_element_type=F32
        ).astype(BF16)
        for k in order:
            l = 2 * x + j
            start_if(l, gy, piece(l, gy, (s3, r3), (j, k - 1), **(to_x(k) if j else to_y(k))))
        for k in order:
            l = 2 * x + j
            start_if(l, gy, piece(l, gy, (s4, r4), (j, 0, k - 1), **(to_y(k) if j else to_x(k))))
    for n in order:
        for j in range(2):
            l, y = (2 * ((x + 4 - n) % 4) + 1, gy) if j else (2 * x, (gy + 4 - n) % 4)
            wait_if(l, y, piece(l, y, (s3, r3), (j, n - 1), gx=gx))
            for k in order:
                start_if(l, y, piece(l, y, (s4, r4), (j, n, k - 1), **(to_y(k) if j else to_x(k))))
    for tap in range(3):
        at = pl.ds(pl.multiple_of((3 * tap + 2 * west) * 256, 256), 256)
        TA[at, :] = jnp.zeros((256, 128), F32)
        RC[at, :] = jnp.zeros((256, 128), F32)
    for n in (0,) + order:
        for k in order:
            for j in range(2):
                if j:
                    l, y = 2 * ((x + 4 - n) % 4) + 1, (gy + 4 - k) % 4
                else:
                    l, y = 2 * ((x + 4 - k) % 4), (gy + 4 - n) % 4
                wait_if(l, y, piece(l, y, (s4, r4), (j, n, k - 1), gx=gx))

    def to_mate(part, start):
        h = core if start else 1 - core
        rows = pl.ds(0, 2304) if part == 0 else pl.ds(256 + 768 * (part - 1), 256)
        view = W.at[h, min(part, 1), rows]
        return remote(view, view, s5.at[part], r5.at[part], gx=gx + 1 - 2 * core)

    for part in range(4):
        to_mate(part, True).start()
        sent.append(to_mate(part, True).wait_send)
    film_in.wait()
    halo_in(1)
    to_mate(0, False).wait_recv()

    row = film[ids[0]]
    mult_a, shift_a, mult_b, shift_b = 1.0 + row[0:1], row[1:2], 1.0 + row[2:3], row[3:4]

    def half(h, block, tap):
        return W[h, block, pl.ds(pl.multiple_of(tap * 256, 256), 256), :]

    def weight(block, tap):
        return jnp.concatenate([half(0, block, tap), half(1, block, tap)], axis=1)

    taps = [(0, 1, 1 + 3), (0, 0, 1), (0, 2, 7)] + [(1, a, 3 * a + 2 - 2 * west) for a in (1, 0, 2)]

    def rows_of(m):
        return pl.ds(pl.multiple_of(m * ROWS, ROWS), ROWS)

    def send_hidden(m):
        return remote(H.at[0, rows_of(m)], H.at[1, rows_of(m)], cs.at[m], cr.at[m], gy=(gy + 2) % 4)

    @pl.loop(0, CHUNKS)
    def _(m):
        r = rows_of(m)
        pre = jnp.zeros((ROWS, 256), F32)
        for col, a, tap in taps:
            pre = pre + jnp.dot(X[col, a, r, :], weight(0, tap), preferred_element_type=F32)
        pre = pre * mult_a + shift_a
        sig = sigmoid(pre)
        H[0, r, :] = (X[0, 1, r, :].astype(F32) + pre * sig).astype(BF16)
        DA[r, :] = mult_a * sig * (1.0 + pre * (1.0 - sig))
        send_hidden(m).start()

    @sent.append
    def _():
        @pl.loop(0, CHUNKS)
        def _(m):
            send_hidden(m).wait_send()

    for part in range(1, 4):
        to_mate(part, False).wait_recv()
    south = gy // 2

    def back_dot(value, tap):
        turned = (((1,), (1,)), ((), ()))
        return lax.dot_general(
            value[:, :128], half(0, 1, tap), turned, preferred_element_type=F32
        ) + lax.dot_general(value[:, 128:], half(1, 1, tap), turned, preferred_element_type=F32)

    @pl.loop(0, CHUNKS)
    def _(m):
        r = rows_of(m)
        ACC[r, :] = jnp.dot(H[0, r, :], weight(1, 4), preferred_element_type=F32)
        FAR[r, :] = jnp.dot(H[0, r, :], weight(1, 1 + 6 * south), preferred_element_type=F32)

    for a in range(3):
        XT[1, a] = X[1, a].T
    cot_out.wait_recv()

    @pl.loop(0, CHUNKS)
    def _(m):
        r = rows_of(m)
        send_hidden(m).wait_recv()
        other = H[1, r, :]
        pre = ACC[r, :] + jnp.dot(other, weight(1, 7 - 6 * south), preferred_element_type=F32)
        pre = pre * mult_b + shift_b
        sig = sigmoid(pre)
        out[r, :] = (H[0, r, :].astype(F32) + pre * sig).astype(BF16)
        up = cot[r, :].astype(F32)
        near_grad = (up * mult_b * sig * (1.0 + pre * (1.0 - sig))).astype(BF16)
        pre = jnp.dot(other, weight(1, 4), preferred_element_type=F32) + FAR[r, :]
        pre = pre * mult_b + shift_b
        sig = sigmoid(pre)
        far_grad = (cot_far[r, :].astype(F32) * mult_b * sig * (1.0 + pre * (1.0 - sig))).astype(BF16)
        back = up + back_dot(near_grad, 4) + back_dot(far_grad, 1 + 6 * south)
        value = back * DA[r, :]
        left, right = value[:, :128], value[:, 128:]
        GA[r, :] = jnp.concatenate(
            [jnp.where(core == 0, left, right), jnp.where(core == 0, right, left)], axis=1
        ).astype(BF16)

    scale = 1.0 / 512.0

    def mate(tap):
        at = pl.ds(pl.multiple_of(tap * 256, 256), 256)
        return remote(TB.at[at], RC.at[at], m1.at[tap], q1.at[tap], gx=gx + 1 - 2 * core)

    def rows72(l, y):
        return pl.ds(pl.multiple_of((l * 4 + y) * 72, 8), 72)

    def empty(l, y):
        number = 4 * l + y
        first = ((number >= 0) & (number <= 2)) | ((number >= 11) & (number <= 13)) | ((number >= 22) & (number <= 23))
        last = ((number >= 8) & (number <= 9)) | ((number >= 18) & (number <= 20)) | (number >= 29)
        return ((west == 0) & first) | ((west == 1) & last)

    def sum_y(k, l):
        return remote(T.at[k - 1, l], RY.at[k - 1, l], m2.at[k - 1, l], q2.at[k - 1, l], gy=(gy + k) % 4)

    def send_rows(a, first, last):
        for col in range(2):
            mate(row_taps[a][col][2]).wait_recv()

        @pl.loop(first, last)
        def _(l):
            for k in order:
                at = rows72(l, (gy + k) % 4)

                @pl.when(jnp.logical_not(empty(l, (gy + k) % 4)))
                def _():
                    T[k - 1, l] = (TA[at, :] + RC[at, :]).astype(BF16)
                    sum_y(k, l).start()

    row_taps = [[(0, a, 3 * a + 1), (1, a, 3 * a + 2 - 2 * west)] for a in range(3)]
    parts = ((0, 2), (2, 5), (5, 8))
    for a in range(3):
        for col, _, tap in row_taps[a]:
            at = pl.ds(pl.multiple_of(tap * 256, 256), 256)
            term = jnp.dot(XT[col, a], GA[...], preferred_element_type=F32) * scale
            TB[at, :] = term[:, 128:]
            mate(tap).start()
            sent.append(mate(tap).wait_send)
            TA[at, :] = term[:, :128]
        if a:
            send_rows(a - 1, *parts[a - 1])
    send_rows(2, *parts[2])

    @sent.append
    def _():
        for k in order:

            @pl.loop(0, 8)
            def _(l):
                @pl.when(jnp.logical_not(empty(l, (gy + k) % 4)))
                def _():
                    sum_y(k, l).wait_send()

    @pl.loop(0, 8)
    def _(l):
        at = rows72(l, gy)
        A2[l] = TA[at, :] + RC[at, :]

    def sum_x(k, h):
        part = pl.ds(4 * h, 4)
        return remote(XB.at[k - 1, part], PX.at[k - 1, part], m3.at[k - 1, h], q3.at[k - 1, h], gx=(gx + 4 * k) % 16)

    def window(xx, h):
        return A2[4 * h : 4 * h + 4, pl.ds(pl.multiple_of(xx * 16, 16), 24), :]

    for h in range(2):
        for k in order:

            @pl.loop(4 * h, 4 * h + 4)
            def _(l):
                @pl.when(jnp.logical_not(empty(l, gy)))
                def _():
                    sum_y(k, l).wait_recv()
                    A2[l] += RY[k - 1, l].astype(F32)

        for k in order:
            XB[k - 1, 4 * h : 4 * h + 4] = window((x + k) % 4, h).astype(BF16)
            sum_x(k, h).start()
            sent.append(sum_x(k, h).wait_send)

    def sum_z(k):
        z = (zid + k) % 16
        return remote(ZB.at[z // 8, z % 8], ZR.at[k], m4.at[k], q4.at[k], **ring(k))

    for h in range(2):
        P = window(x, h)
        for k in order:
            sum_x(k, h).wait_recv()
            P = P + PX[k - 1, 4 * h : 4 * h + 4].astype(F32)
        PP[4 * h : 4 * h + 4] = P
        ZB[0, 4 * h : 4 * h + 4] = P[:, 0:16].astype(BF16)
        ZB[1, 4 * h : 4 * h + 4] = P[:, 8:24].astype(BF16)
        for k in far_first:

            @pl.when((zid + k) % 8 // 4 == h)
            def _():
                sum_z(k).start()

    for k in far_first:
        sent.append(sum_z(k).wait_send)
    total = PP[lead, pl.ds(pl.multiple_of(zh * 8, 8), 16), :]
    for k in far_first[::-1]:
        sum_z(k).wait_recv()
        total = total + ZR[k].astype(F32)
    RR[core] = total
    swap = remote(RR.at[core], RR.at[core], m5, q5, gx=gx + 1 - 2 * core)
    swap_in = remote(RR.at[1 - core], RR.at[1 - core], m5, q5, gx=gx + 1 - 2 * core)
    swap.start()
    sent.append(swap.wait_send)
    swap_in.wait_recv()
    for j in range(9):
        grad[j : j + 1, :] = RR[(j + core) % 2, pl.ds(2 * x + zh + (9 * core + j) // 2, 1), :]
    finish()


def shards(inputs, lead_ids, film, flat_weights, cotangent):
    padded = jnp.pad(flat_weights.reshape(2, 9, 128), ((0, 0), (0, 7), (0, 0)))
    vmem = pl.BlockSpec(memory_space=pltpu.VMEM)
    hbm = pl.BlockSpec(memory_space=pltpu.HBM)
    outputs, total = pl.pallas_call(
        step_kernel,
        out_shape=(jax.ShapeDtypeStruct((512, 256), BF16), jax.ShapeDtypeStruct((9, 128), F32)),
        in_specs=[pl.BlockSpec(memory_space=pltpu.SMEM), vmem, hbm, hbm, hbm],
        out_specs=(vmem, vmem),
        scratch_shapes=[
            pltpu.VMEM((2, 2, 2304, 128), BF16),
            pltpu.VMEM((2, 8, 2, 16, 128), BF16),
            pltpu.VMEM((2, 2, 4, 2, 2, 16, 128), BF16),
            pltpu.VMEM((2, 3, 512, 256), BF16),
            pltpu.VMEM((2, 3, 256, 512), BF16),
            pltpu.VMEM((2, 512, 256), BF16),
            pltpu.VMEM((512, 256), BF16),
            pltpu.VMEM((512, 256), F32),
            pltpu.VMEM((512, 256), F32),
            pltpu.VMEM((512, 256), F32),
            pltpu.VMEM((2304, 128), F32),
            pltpu.VMEM((2304, 128), F32),
            pltpu.VMEM((2304, 128), F32),
            pltpu.VMEM((3, 8, 72, 128), BF16),
            pltpu.VMEM((3, 8, 72, 128), BF16),
            pltpu.VMEM((8, 72, 128), F32),
            pltpu.VMEM((3, 8, 24, 128), BF16),
            pltpu.VMEM((3, 8, 24, 128), BF16),
            pltpu.VMEM((8, 24, 128), F32),
            pltpu.VMEM((2, 8, 16, 128), BF16),
            pltpu.VMEM((16, 16, 128), BF16),
            pltpu.VMEM((2, 16, 128), F32),
            pltpu.VMEM((360, 4, 256), F32),
            pltpu.VMEM((512, 256), BF16),
            pltpu.VMEM((512, 256), BF16),
            DMA((3,)),
            DMA((4, 2)), DMA((4, 2)),
            DMA((CHUNKS,)), DMA((CHUNKS,)),
            DMA(()), DMA(()),
            DMA((16,)), DMA((16,)),
            DMA((8,)), DMA((2, 4)), DMA(()), DMA(()),
            DMA((2, 3)), DMA((2, 3)),
            DMA((2, 4, 3)), DMA((2, 4, 3)),
            DMA((4,)), DMA((4,)),
            DMA((9,)), DMA((9,)),
            DMA((3, 8)), DMA((3, 8)),
            DMA((3, 2)), DMA((3, 2)),
            DMA((16,)), DMA((16,)),
            DMA(()), DMA(()),
        ],
        compiler_params=pltpu.CompilerParams(
            collective_id=0, has_side_effects=True, vmem_limit_bytes=50 << 20
        ),
    )(lead_ids, padded, inputs.reshape(512, 256), film, cotangent.reshape(512, 256))
    return (outputs.reshape(inputs.shape), total.reshape(-1))


def solution(mesh):
    return jax.shard_map(
        shards,
        mesh=mesh,
        in_specs=(
            P("lead", "gy", "gx", None),
            P("lead"),
            P(),
            P(None, ("lead", "gy", "gx")),
            P("lead", "gy", "gx", None),
        ),
        out_specs=(P("lead", "gy", "gx", None), P(("lead", "gy", "gx"))),
        check_vma=False,
    )
```

```python
import jax
import jax.numpy as jnp
from jax import lax
from jax.experimental import pallas as pl
from jax.experimental.pallas import tpu as pltpu
from jax.sharding import PartitionSpec as P

MESH = pl.DeviceIdType.MESH
DMA = pltpu.SemaphoreType.DMA
F32, BF16 = jnp.float32, jnp.bfloat16


def place():
    lead, gy, gx = lax.axis_index("lead"), lax.axis_index("gy"), lax.axis_index("gx")
    return lead, gy, gx, gx // 4, (gx // 2) % 2, gx % 2


def remote(src, dst, send_sem, recv_sem, **where):
    return pltpu.make_async_remote_copy(
        src_ref=src, dst_ref=dst, send_sem=send_sem, recv_sem=recv_sem, device_id=where, device_id_type=MESH
    )


def greet():
    lead, gy, gx, x, zh, core = place()
    barrier = pltpu.get_barrier_semaphore()
    first = gy - gy % 2

    def hello(**where):
        pl.semaphore_signal(barrier, inc=1, device_id=where, device_id_type=MESH)

    for k in range(1, 16):
        hello(**ring(k))
    hello(gy=(gy + 2) % 4)
    hello(gy=3 - gy)
    for k in range(1, 16):
        hello(gy=first + (gy % 2 + k // 8) % 2, gx=(x + (k // 2) % 4) % 4 * 4 + zh * 2 + (core + k) % 2)
    pl.semaphore_wait(barrier, 32)


def ring(k):
    lead, gy, gx, x, zh, core = place()
    z = (zh * 8 + lead + k) % 16
    return {"lead": z % 8, "gx": x * 4 + (z // 8) * 2 + core}


ROWS = 128
CHUNKS = 4


def group(lead, gy):
    return pl.ds(pl.multiple_of((lead * 2 + gy // 2) * 144, 16), 144)


def quarter(x):
    return pl.ds(pl.multiple_of(x * 576, 64), 576)


def sigmoid(v):
    return 1.0 / (1.0 + jnp.exp(-v))


def step_kernel(
    ids, w_ref, x_hbm, film_hbm, cot_hbm, out, grad,
    W, R, BD, X, XT, H, GA, DA, ACC, FAR, TA, TB, RC, T, RY, A2, XB, PX, PP, ZB, ZR, RR, film, cot, cot_far,
    ls, hs, hr, cs, cr, es, er, s1, r1, s2, r2, s3, r3, s4, r4, s5, r5, m1, q1, m2, q2, m3, q3, m4, q4, m5, q5,
):
    lead, gy, gx, x, zh, core = place()
    zid = zh * 8 + lead
    west = x // 2
    block = gy % 2
    pair = gy - block
    sent = []

    def finish():
        for wait in sent:
            wait()

    x_in = pltpu.make_async_copy(x_hbm, X.at[0, 1], ls.at[0])
    film_in = pltpu.make_async_copy(film_hbm, film, ls.at[1])
    cot_in = pltpu.make_async_copy(cot_hbm, cot, ls.at[2])
    x_in.start()
    film_in.start()
    cot_in.start()
    R[zh, lead] = w_ref[...]
    x_in.wait()
    greet()

    far_first = (8, 7, 9, 6, 10, 5, 11, 4, 12, 3, 13, 2, 14, 1, 15)

    def needed(l, y):
        number = 2 * l + y // 2
        inside = ((number >= 1) & (number <= 3)) | ((number >= 7) & (number <= 8)) | ((number >= 12) & (number <= 14))
        return (y % 2 == 0) | inside

    def spread(k, both):
        own = R.at[zh, lead] if both else R.at[zh, lead, 0]
        return remote(own, own, s1.at[k], r1.at[k], **ring(k))

    def spread_in(k, both):
        z = (zid + 16 - k) % 16
        own = R.at[z // 8, z % 8] if both else R.at[z // 8, z % 8, 0]
        return remote(own, own, s1.at[k], r1.at[k], **ring(k))

    def each_spread(act):
        for both in (True, False):

            @pl.when(needed(lead, pair + 1) if both else jnp.logical_not(needed(lead, pair + 1)))
            def _():
                for k in far_first:
                    act(spread(k, both))

    each_spread(lambda copy: copy.start())
    sent.append(lambda: each_spread(lambda copy: copy.wait_send()))
    def halo(col, up):
        return remote(
            X.at[col, 1], X.at[col, 0 if up else 2], hs.at[col, int(up)], hr.at[col, int(up)],
            gy=(gy + (1 if up else 3)) % 4,
        )

    def across(part):
        rows = pl.ds(256 * part, 256)
        return remote(X.at[0, 1, rows], X.at[1, 1, rows], hs.at[2, part], hr.at[2, part], gx=(gx + 8) % 16)

    def corner(part, up):
        rows = pl.ds(256 * part, 256)
        return remote(
            X.at[1, 1, rows], X.at[1, 0 if up else 2, rows], hs.at[1 + 2 * part, int(up)], hr.at[1 + 2 * part, int(up)],
            gy=(gy + (1 if up else 3)) % 4,
        )

    has = {True: gy < 3, False: gy > 0}
    gets = {True: gy > 0, False: gy < 3}
    for part in range(2):
        across(part).start()
        sent.append(across(part).wait_send)

    def halo_out():
        for up in (True, False):

            @pl.when(has[up])
            def _():
                halo(0, up).start()

    def corner_out(part):
        across(part).wait_recv()
        for up in (True, False):

            @pl.when(has[up])
            def _():
                corner(part, up).start()

    @sent.append
    def _():
        for up in (True, False):

            @pl.when(has[up])
            def _():
                halo(0, up).wait_send()
                corner(0, up).wait_send()
                corner(1, up).wait_send()

    def halo_in(col):
        for up in (True, False):

            @pl.when(gets[up])
            def _():
                if col == 0:
                    halo(0, up).wait_recv()
                else:
                    corner(0, up).wait_recv()
                    corner(1, up).wait_recv()

            @pl.when(jnp.logical_not(gets[up]))
            def _():
                X[col, 0 if up else 2] = jnp.zeros((512, 256), BF16)

    halo_out()
    corner_out(0)
    XT[0, 1] = X[0, 1].T
    for k in far_first[::-1]:
        z = (zid + 16 - k) % 16
        for both in (True, False):

            @pl.when(needed(z % 8, pair + 1) if both else jnp.logical_not(needed(z % 8, pair + 1)))
            def _():
                spread_in(k, both).wait_recv()

    def gather(k):
        y, xx = (block + k // 8) % 2, (x + (k // 2) % 4) % 4
        return remote(
            R.at[:, pl.ds(2 * xx, 2), y], BD.at[block, x, core], s2.at[k], r2.at[block, x, core],
            gy=pair + y, gx=xx * 4 + zh * 2 + (core + k) % 2,
        )

    def gather_in(k):
        y, xx, c = (block + k // 8) % 2, (x + (k // 2) % 4) % 4, (core + k) % 2
        return remote(R.at[:, pl.ds(2 * x, 2), 0], BD.at[y, xx, c], s2.at[k], r2.at[y, xx, c], gy=gy, gx=gx)

    for k in range(1, 16):
        gather(k).start()
        sent.append(gather(k).wait_send)
    BD[block, x, core] = R[:, pl.ds(2 * x, 2), block]
    row = lax.broadcasted_iota(jnp.int32, (144, 512), 0) * 2 + core
    column = lax.broadcasted_iota(jnp.int32, (144, 512), 1)
    owner = (row * 57) >> 9
    place_of = ((owner >> 2) * 2 + (owner & 1)) * 2 + ((owner >> 1) & 1)
    pick = (column == place_of * 16 + (row - owner * 9)).astype(F32).astype(BF16)
    corner_out(1)
    halo_in(0)
    XT[0, 0] = X[0, 0].T
    XT[0, 2] = X[0, 2].T
    for k in range(1, 16):
        gather_in(k).wait_recv()

    def piece(l, y, sems, slot, **where):
        part = W.at[core, y % 2, group(l, y)]
        return remote(part, part, sems[0].at[slot], sems[1].at[slot], **where)

    def start_if(l, y, copy):
        @pl.when(needed(l, y))
        def _():
            copy.start()

        @sent.append
        def _():
            @pl.when(needed(l, y))
            def _():
                copy.wait_send()

    def wait_if(l, y, copy):
        @pl.when(needed(l, y))
        def _():
            copy.wait_recv()

    order = (1, 3, 2)

    def to_y(k):
        return {"gy": (gy + k) % 4}

    def to_x(k):
        return {"gx": (gx + 4 * k) % 16}

    for j in range(2):
        W[core, block, group(2 * x + j, gy), :] = jnp.dot(
            pick, BD[:, :, :, :, j].reshape(512, 128), preferred_element_type=F32
        ).astype(BF16)
        for k in order:
            l = 2 * x + j
            start_if(l, gy, piece(l, gy, (s3, r3), (j, k - 1), **(to_x(k) if j else to_y(k))))
        for k in order:
            l = 2 * x + j
            start_if(l, gy, piece(l, gy, (s4, r4), (j, 0, k - 1), **(to_y(k) if j else to_x(k))))
    for n in order:
        for j in range(2):
            l, y = (2 * ((x + 4 - n) % 4) + 1, gy) if j else (2 * x, (gy + 4 - n) % 4)
            wait_if(l, y, piece(l, y, (s3, r3), (j, n - 1), gx=gx))
            for k in order:
                start_if(l, y, piece(l, y, (s4, r4), (j, n, k - 1), **(to_y(k) if j else to_x(k))))
    cot_in.wait()
    cot_out = remote(cot, cot_far, es, er, gy=(gy + 2) % 4)
    cot_out.start()
    sent.append(cot_out.wait_send)
    for tap in range(3):
        at = pl.ds(pl.multiple_of((3 * tap + 2 * west) * 256, 256), 256)
        TA[at, :] = jnp.zeros((256, 128), F32)
        RC[at, :] = jnp.zeros((256, 128), F32)
    for n in (0,) + order:
        for k in order:
            for j in range(2):
                if j:
                    l, y = 2 * ((x + 4 - n) % 4) + 1, (gy + 4 - k) % 4
                else:
                    l, y = 2 * ((x + 4 - k) % 4), (gy + 4 - n) % 4
                wait_if(l, y, piece(l, y, (s4, r4), (j, n, k - 1), gx=gx))

    def to_mate(part, start):
        h = core if start else 1 - core
        rows = pl.ds(0, 2304) if part == 0 else pl.ds(256 + 768 * (part - 1), 256)
        view = W.at[h, min(part, 1), rows]
        return remote(view, view, s5.at[part], r5.at[part], gx=gx + 1 - 2 * core)

    for part in range(4):
        to_mate(part, True).start()
        sent.append(to_mate(part, True).wait_send)
    film_in.wait()
    halo_in(1)
    to_mate(0, False).wait_recv()

    row = film[ids[0]]
    mult_a, shift_a, mult_b, shift_b = 1.0 + row[0:1], row[1:2], 1.0 + row[2:3], row[3:4]

    def half(h, block, tap):
        return W[h, block, pl.ds(pl.multiple_of(tap * 256, 256), 256), :]

    def weight(block, tap):
        return jnp.concatenate([half(0, block, tap), half(1, block, tap)], axis=1)

    taps = [(0, 1, 1 + 3), (0, 0, 1), (0, 2, 7)] + [(1, a, 3 * a + 2 - 2 * west) for a in (1, 0, 2)]

    def rows_of(m):
        return pl.ds(pl.multiple_of(m * ROWS, ROWS), ROWS)

    def send_hidden(m):
        return remote(H.at[0, rows_of(m)], H.at[1, rows_of(m)], cs.at[m], cr.at[m], gy=(gy + 2) % 4)

    @pl.loop(0, CHUNKS)
    def _(m):
        r = rows_of(m)
        pre = jnp.zeros((ROWS, 256), F32)
        for col, a, tap in taps:
            pre = pre + jnp.dot(X[col, a, r, :], weight(0, tap), preferred_element_type=F32)
        pre = pre * mult_a + shift_a
        sig = sigmoid(pre)
        H[0, r, :] = (X[0, 1, r, :].astype(F32) + pre * sig).astype(BF16)
        DA[r, :] = mult_a * sig * (1.0 + pre * (1.0 - sig))
        send_hidden(m).start()

    @sent.append
    def _():
        @pl.loop(0, CHUNKS)
        def _(m):
            send_hidden(m).wait_send()

    for part in range(1, 4):
        to_mate(part, False).wait_recv()
    south = gy // 2

    def back_dot(value, tap):
        turned = (((1,), (1,)), ((), ()))
        return lax.dot_general(
            value[:, :128], half(0, 1, tap), turned, preferred_element_type=F32
        ) + lax.dot_general(value[:, 128:], half(1, 1, tap), turned, preferred_element_type=F32)

    @pl.loop(0, CHUNKS)
    def _(m):
        r = rows_of(m)
        ACC[r, :] = jnp.dot(H[0, r, :], weight(1, 4), preferred_element_type=F32)
        FAR[r, :] = jnp.dot(H[0, r, :], weight(1, 1 + 6 * south), preferred_element_type=F32)

    for a in range(3):
        XT[1, a] = X[1, a].T
    cot_out.wait_recv()

    @pl.loop(0, CHUNKS)
    def _(m):
        r = rows_of(m)
        send_hidden(m).wait_recv()
        other = H[1, r, :]
        pre = ACC[r, :] + jnp.dot(other, weight(1, 7 - 6 * south), preferred_element_type=F32)
        pre = pre * mult_b + shift_b
        sig = sigmoid(pre)
        out[r, :] = (H[0, r, :].astype(F32) + pre * sig).astype(BF16)
        up = cot[r, :].astype(F32)
        near_grad = (up * mult_b * sig * (1.0 + pre * (1.0 - sig))).astype(BF16)
        pre = jnp.dot(other, weight(1, 4), preferred_element_type=F32) + FAR[r, :]
        pre = pre * mult_b + shift_b
        sig = sigmoid(pre)
        far_grad = (cot_far[r, :].astype(F32) * mult_b * sig * (1.0 + pre * (1.0 - sig))).astype(BF16)
        back = up + back_dot(near_grad, 4) + back_dot(far_grad, 1 + 6 * south)
        value = back * DA[r, :]
        left, right = value[:, :128], value[:, 128:]
        GA[r, :] = jnp.concatenate(
            [jnp.where(core == 0, left, right), jnp.where(core == 0, right, left)], axis=1
        ).astype(BF16)

    scale = 1.0 / 512.0

    def mate(tap):
        at = pl.ds(pl.multiple_of(tap * 256, 256), 256)
        return remote(TB.at[at], RC.at[at], m1.at[tap], q1.at[tap], gx=gx + 1 - 2 * core)

    def rows72(l, y):
        return pl.ds(pl.multiple_of((l * 4 + y) * 72, 8), 72)

    def empty(l, y):
        number = 4 * l + y
        first = ((number >= 0) & (number <= 2)) | ((number >= 11) & (number <= 13)) | ((number >= 22) & (number <= 23))
        last = ((number >= 8) & (number <= 9)) | ((number >= 18) & (number <= 20)) | (number >= 29)
        return ((west == 0) & first) | ((west == 1) & last)

    def sum_y(k, l):
        return remote(T.at[k - 1, l], RY.at[k - 1, l], m2.at[k - 1, l], q2.at[k - 1, l], gy=(gy + k) % 4)

    def send_rows(a, first, last):
        for col in range(2):
            mate(row_taps[a][col][2]).wait_recv()

        @pl.loop(first, last)
        def _(l):
            for k in order:
                at = rows72(l, (gy + k) % 4)

                @pl.when(jnp.logical_not(empty(l, (gy + k) % 4)))
                def _():
                    T[k - 1, l] = (TA[at, :] + RC[at, :]).astype(BF16)
                    sum_y(k, l).start()

    row_taps = [[(0, a, 3 * a + 1), (1, a, 3 * a + 2 - 2 * west)] for a in range(3)]
    parts = ((0, 2), (2, 5), (5, 8))
    for a in range(3):
        for col, _, tap in row_taps[a]:
            at = pl.ds(pl.multiple_of(tap * 256, 256), 256)
            term = jnp.dot(XT[col, a], GA[...], preferred_element_type=F32) * scale
            TB[at, :] = term[:, 128:]
            mate(tap).start()
            sent.append(mate(tap).wait_send)
            TA[at, :] = term[:, :128]
        if a:
            send_rows(a - 1, *parts[a - 1])
    send_rows(2, *parts[2])

    @sent.append
    def _():
        for k in order:

            @pl.loop(0, 8)
            def _(l):
                @pl.when(jnp.logical_not(empty(l, (gy + k) % 4)))
                def _():
                    sum_y(k, l).wait_send()

    @pl.loop(0, 8)
    def _(l):
        at = rows72(l, gy)
        A2[l] = TA[at, :] + RC[at, :]

    def sum_x(k, h):
        part = pl.ds(4 * h, 4)
        return remote(XB.at[k - 1, part], PX.at[k - 1, part], m3.at[k - 1, h], q3.at[k - 1, h], gx=(gx + 4 * k) % 16)

    def window(xx, h):
        return A2[4 * h : 4 * h + 4, pl.ds(pl.multiple_of(xx * 16, 16), 24), :]

    for h in range(2):
        for k in order:

            @pl.loop(4 * h, 4 * h + 4)
            def _(l):
                @pl.when(jnp.logical_not(empty(l, gy)))
                def _():
                    sum_y(k, l).wait_recv()
                    A2[l] += RY[k - 1, l].astype(F32)

        for k in order:
            XB[k - 1, 4 * h : 4 * h + 4] = window((x + k) % 4, h).astype(BF16)
            sum_x(k, h).start()
            sent.append(sum_x(k, h).wait_send)

    def sum_z(k):
        z = (zid + k) % 16
        return remote(ZB.at[z // 8, z % 8], ZR.at[k], m4.at[k], q4.at[k], **ring(k))

    for h in range(2):
        P = window(x, h)
        for k in order:
            sum_x(k, h).wait_recv()
            P = P + PX[k - 1, 4 * h : 4 * h + 4].astype(F32)
        PP[4 * h : 4 * h + 4] = P
        ZB[0, 4 * h : 4 * h + 4] = P[:, 0:16].astype(BF16)
        ZB[1, 4 * h : 4 * h + 4] = P[:, 8:24].astype(BF16)
        for k in far_first:

            @pl.when((zid + k) % 8 // 4 == h)
            def _():
                sum_z(k).start()

    for k in far_first:
        sent.append(sum_z(k).wait_send)
    total = PP[lead, pl.ds(pl.multiple_of(zh * 8, 8), 16), :]
    for k in far_first[::-1]:
        sum_z(k).wait_recv()
        total = total + ZR[k].astype(F32)
    RR[core] = total
    swap = remote(RR.at[core], RR.at[core], m5, q5, gx=gx + 1 - 2 * core)
    swap_in = remote(RR.at[1 - core], RR.at[1 - core], m5, q5, gx=gx + 1 - 2 * core)
    swap.start()
    sent.append(swap.wait_send)
    swap_in.wait_recv()
    for j in range(9):
        grad[j : j + 1, :] = RR[(j + core) % 2, pl.ds(2 * x + zh + (9 * core + j) // 2, 1), :]
    finish()


def shards(inputs, lead_ids, film, flat_weights, cotangent):
    padded = jnp.pad(flat_weights.reshape(2, 9, 128), ((0, 0), (0, 7), (0, 0)))
    vmem = pl.BlockSpec(memory_space=pltpu.VMEM)
    hbm = pl.BlockSpec(memory_space=pltpu.HBM)
    outputs, total = pl.pallas_call(
        step_kernel,
        out_shape=(jax.ShapeDtypeStruct((512, 256), BF16), jax.ShapeDtypeStruct((9, 128), F32)),
        in_specs=[pl.BlockSpec(memory_space=pltpu.SMEM), vmem, hbm, hbm, hbm],
        out_specs=(vmem, vmem),
        scratch_shapes=[
            pltpu.VMEM((2, 2, 2304, 128), BF16),
            pltpu.VMEM((2, 8, 2, 16, 128), BF16),
            pltpu.VMEM((2, 4, 2, 2, 2, 16, 128), BF16),
            pltpu.VMEM((2, 3, 512, 256), BF16),
            pltpu.VMEM((2, 3, 256, 512), BF16),
            pltpu.VMEM((2, 512, 256), BF16),
            pltpu.VMEM((512, 256), BF16),
            pltpu.VMEM((512, 256), F32),
            pltpu.VMEM((512, 256), F32),
            pltpu.VMEM((512, 256), F32),
            pltpu.VMEM((2304, 128), F32),
            pltpu.VMEM((2304, 128), F32),
            pltpu.VMEM((2304, 128), F32),
            pltpu.VMEM((3, 8, 72, 128), BF16),
            pltpu.VMEM((3, 8, 72, 128), BF16),
            pltpu.VMEM((8, 72, 128), F32),
            pltpu.VMEM((3, 8, 24, 128), BF16),
            pltpu.VMEM((3, 8, 24, 128), BF16),
            pltpu.VMEM((8, 24, 128), F32),
            pltpu.VMEM((2, 8, 16, 128), BF16),
            pltpu.VMEM((16, 16, 128), BF16),
            pltpu.VMEM((2, 16, 128), F32),
            pltpu.VMEM((360, 4, 256), F32),
            pltpu.VMEM((512, 256), BF16),
            pltpu.VMEM((512, 256), BF16),
            DMA((3,)),
            DMA((4, 2)), DMA((4, 2)),
            DMA((CHUNKS,)), DMA((CHUNKS,)),
            DMA(()), DMA(()),
            DMA((16,)), DMA((16,)),
            DMA((16,)), DMA((2, 4, 2)),
            DMA((2, 3)), DMA((2, 3)),
            DMA((2, 4, 3)), DMA((2, 4, 3)),
            DMA((4,)), DMA((4,)),
            DMA((9,)), DMA((9,)),
            DMA((3, 8)), DMA((3, 8)),
            DMA((3, 2)), DMA((3, 2)),
            DMA((16,)), DMA((16,)),
            DMA(()), DMA(()),
        ],
        compiler_params=pltpu.CompilerParams(
            collective_id=0, has_side_effects=True, vmem_limit_bytes=50 << 20
        ),
    )(lead_ids, padded, inputs.reshape(512, 256), film, cotangent.reshape(512, 256))
    return (outputs.reshape(inputs.shape), total.reshape(-1))


def solution(mesh):
    return jax.shard_map(
        shards,
        mesh=mesh,
        in_specs=(
            P("lead", "gy", "gx", None),
            P("lead"),
            P(),
            P(None, ("lead", "gy", "gx")),
            P("lead", "gy", "gx", None),
        ),
        out_specs=(P("lead", "gy", "gx", None), P(("lead", "gy", "gx"))),
        check_vma=False,
    )
```

```python
import jax
import jax.numpy as jnp
from jax import lax
from jax.experimental import pallas as pl
from jax.experimental.pallas import tpu as pltpu
from jax.sharding import PartitionSpec as P

MESH = pl.DeviceIdType.MESH
DMA = pltpu.SemaphoreType.DMA
F32, BF16 = jnp.float32, jnp.bfloat16


def place():
    lead, gy, gx = lax.axis_index("lead"), lax.axis_index("gy"), lax.axis_index("gx")
    return lead, gy, gx, gx // 4, (gx // 2) % 2, gx % 2


def remote(src, dst, send_sem, recv_sem, **where):
    return pltpu.make_async_remote_copy(
        src_ref=src, dst_ref=dst, send_sem=send_sem, recv_sem=recv_sem, device_id=where, device_id_type=MESH
    )


def greet():
    lead, gy, gx, x, zh, core = place()
    barrier = pltpu.get_barrier_semaphore()
    first = gy - gy % 2

    def hello(**where):
        pl.semaphore_signal(barrier, inc=1, device_id=where, device_id_type=MESH)

    for k in range(1, 16):
        hello(**ring(k))
    hello(gy=(gy + 2) % 4)
    hello(gy=3 - gy)
    for k in range(1, 16):
        hello(gy=first + (gy % 2 + k // 8) % 2, gx=(x + (k // 2) % 4) % 4 * 4 + zh * 2 + (core + k) % 2)
    pl.semaphore_wait(barrier, 32)


def ring(k):
    lead, gy, gx, x, zh, core = place()
    z = (zh * 8 + lead + k) % 16
    return {"lead": z % 8, "gx": x * 4 + (z // 8) * 2 + core}


ROWS = 128
CHUNKS = 4


def group(lead, gy):
    return pl.ds(pl.multiple_of((lead * 2 + gy // 2) * 144, 16), 144)


def quarter(x):
    return pl.ds(pl.multiple_of(x * 576, 64), 576)


def sigmoid(v):
    return 1.0 / (1.0 + jnp.exp(-v))


def step_kernel(
    ids, w_ref, x_hbm, film_hbm, cot_hbm, out, grad,
    W, R, BD, X, XT, H, GA, DA, ACC, FAR, TA, TB, RC, T, RY, A2, XB, PX, PP, ZB, ZR, RR, film, cot, cot_far,
    ls, hs, hr, cs, cr, es, er, s1, r1, s2, r2, s3, r3, s4, r4, s5, r5, m1, q1, m2, q2, m3, q3, m4, q4, m5, q5,
):
    lead, gy, gx, x, zh, core = place()
    zid = zh * 8 + lead
    west = x // 2
    block = gy % 2
    pair = gy - block
    sent = []

    def finish():
        for wait in sent:
            wait()

    x_in = pltpu.make_async_copy(x_hbm, X.at[0, 1], ls.at[0])
    film_in = pltpu.make_async_copy(film_hbm, film, ls.at[1])
    cot_in = pltpu.make_async_copy(cot_hbm, cot, ls.at[2])
    x_in.start()
    film_in.start()
    cot_in.start()
    R[zh, lead] = w_ref[...]
    x_in.wait()
    greet()

    far_first = (8, 7, 9, 6, 10, 5, 11, 4, 12, 3, 13, 2, 14, 1, 15)

    def needed(l, y):
        number = 2 * l + y // 2
        inside = ((number >= 1) & (number <= 3)) | ((number >= 7) & (number <= 8)) | ((number >= 12) & (number <= 14))
        return (y % 2 == 0) | inside

    def spread(k, both):
        own = R.at[zh, lead] if both else R.at[zh, lead, 0]
        return remote(own, own, s1.at[k], r1.at[k], **ring(k))

    def spread_in(k, both):
        z = (zid + 16 - k) % 16
        own = R.at[z // 8, z % 8] if both else R.at[z // 8, z % 8, 0]
        return remote(own, own, s1.at[k], r1.at[k], **ring(k))

    def each_spread(act):
        for both in (True, False):

            @pl.when(needed(lead, pair + 1) if both else jnp.logical_not(needed(lead, pair + 1)))
            def _():
                for k in far_first:
                    act(spread(k, both))

    each_spread(lambda copy: copy.start())
    sent.append(lambda: each_spread(lambda copy: copy.wait_send()))
    def halo(col, up):
        return remote(
            X.at[col, 1], X.at[col, 0 if up else 2], hs.at[col, int(up)], hr.at[col, int(up)],
            gy=(gy + (1 if up else 3)) % 4,
        )

    def across(part):
        rows = pl.ds(256 * part, 256)
        return remote(X.at[0, 1, rows], X.at[1, 1, rows], hs.at[2, part], hr.at[2, part], gx=(gx + 8) % 16)

    def corner(part, up):
        rows = pl.ds(256 * part, 256)
        return remote(
            X.at[1, 1, rows], X.at[1, 0 if up else 2, rows], hs.at[1 + 2 * part, int(up)], hr.at[1 + 2 * part, int(up)],
            gy=(gy + (1 if up else 3)) % 4,
        )

    has = {True: gy < 3, False: gy > 0}
    gets = {True: gy > 0, False: gy < 3}
    for part in range(2):
        across(part).start()
        sent.append(across(part).wait_send)

    def halo_out():
        for up in (True, False):

            @pl.when(has[up])
            def _():
                halo(0, up).start()

    def corner_out(part):
        across(part).wait_recv()
        for up in (True, False):

            @pl.when(has[up])
            def _():
                corner(part, up).start()

    @sent.append
    def _():
        for up in (True, False):

            @pl.when(has[up])
            def _():
                halo(0, up).wait_send()
                corner(0, up).wait_send()
                corner(1, up).wait_send()

    def halo_in(col):
        for up in (True, False):

            @pl.when(gets[up])
            def _():
                if col == 0:
                    halo(0, up).wait_recv()
                else:
                    corner(0, up).wait_recv()
                    corner(1, up).wait_recv()

            @pl.when(jnp.logical_not(gets[up]))
            def _():
                X[col, 0 if up else 2] = jnp.zeros((512, 256), BF16)

    halo_out()
    corner_out(0)
    XT[0, 1] = X[0, 1].T
    for k in far_first[::-1]:
        z = (zid + 16 - k) % 16
        for both in (True, False):

            @pl.when(needed(z % 8, pair + 1) if both else jnp.logical_not(needed(z % 8, pair + 1)))
            def _():
                spread_in(k, both).wait_recv()

    def gather(k):
        y, xx = (block + k // 8) % 2, (x + (k // 2) % 4) % 4
        return remote(
            R.at[:, pl.ds(2 * xx, 2), y], BD.at[block, x, core], s2.at[k], r2.at[block, x, core],
            gy=pair + y, gx=xx * 4 + zh * 2 + (core + k) % 2,
        )

    def gather_in(k):
        y, xx, c = (block + k // 8) % 2, (x + (k // 2) % 4) % 4, (core + k) % 2
        return remote(R.at[:, pl.ds(2 * x, 2), 0], BD.at[y, xx, c], s2.at[k], r2.at[y, xx, c], gy=gy, gx=gx)

    for k in range(1, 16):
        gather(k).start()
        sent.append(gather(k).wait_send)
    BD[block, x, core] = R[:, pl.ds(2 * x, 2), block]
    row = lax.broadcasted_iota(jnp.int32, (144, 512), 0) * 2 + core
    column = lax.broadcasted_iota(jnp.int32, (144, 512), 1)
    owner = (row * 57) >> 9
    place_of = ((owner >> 2) * 2 + (owner & 1)) * 2 + ((owner >> 1) & 1)
    pick = (column == place_of * 16 + (row - owner * 9)).astype(F32).astype(BF16)
    corner_out(1)
    halo_in(0)
    XT[0, 0] = X[0, 0].T
    XT[0, 2] = X[0, 2].T
    for k in range(1, 16):
        gather_in(k).wait_recv()

    def piece(l, y, sems, slot, **where):
        part = W.at[core, y % 2, group(l, y)]
        return remote(part, part, sems[0].at[slot], sems[1].at[slot], **where)

    def wanted(l, y, side):
        number = 2 * l + y // 2
        west_skips = (side == 0) & ((number == 0) | (number == 6) | (number == 11))
        east_skips = (side == 1) & ((number == 4) | (number == 9) | (number == 15))
        return needed(l, y) & jnp.logical_not((y % 2 == 0) & (west_skips | east_skips))

    def start_if(l, y, copy, side):
        @pl.when(wanted(l, y, side))
        def _():
            copy.start()

        @sent.append
        def _():
            @pl.when(wanted(l, y, side))
            def _():
                copy.wait_send()

    def wait_if(l, y, copy, side):
        @pl.when(wanted(l, y, side))
        def _():
            copy.wait_recv()

    order = (1, 3, 2)

    def to_y(k):
        return {"gy": (gy + k) % 4}

    def to_x(k):
        return {"gx": (gx + 4 * k) % 16}

    for j in range(2):
        W[core, block, group(2 * x + j, gy), :] = jnp.dot(
            pick, BD[:, :, :, :, j].reshape(512, 128), preferred_element_type=F32
        ).astype(BF16)
        for k in order:
            l = 2 * x + j
            start_if(l, gy, piece(l, gy, (s3, r3), (j, k - 1), **(to_x(k) if j else to_y(k))), (x + k) % 4 // 2 if j else 2)
        for k in order:
            l = 2 * x + j
            start_if(l, gy, piece(l, gy, (s4, r4), (j, 0, k - 1), **(to_y(k) if j else to_x(k))), west if j else (x + k) % 4 // 2)
    for n in order:
        for j in range(2):
            l, y = (2 * ((x + 4 - n) % 4) + 1, gy) if j else (2 * x, (gy + 4 - n) % 4)
            wait_if(l, y, piece(l, y, (s3, r3), (j, n - 1), gx=gx), west if j else 2)
            for k in order:
                start_if(l, y, piece(l, y, (s4, r4), (j, n, k - 1), **(to_y(k) if j else to_x(k))), west if j else (x + k) % 4 // 2)
    cot_in.wait()
    cot_out = remote(cot, cot_far, es, er, gy=(gy + 2) % 4)
    cot_out.start()
    sent.append(cot_out.wait_send)
    for tap in range(3):
        at = pl.ds(pl.multiple_of((3 * tap + 2 * west) * 256, 256), 256)
        TA[at, :] = jnp.zeros((256, 128), F32)
        RC[at, :] = jnp.zeros((256, 128), F32)
    for n in (0,) + order:
        for k in order:
            for j in range(2):
                if j:
                    l, y = 2 * ((x + 4 - n) % 4) + 1, (gy + 4 - k) % 4
                else:
                    l, y = 2 * ((x + 4 - k) % 4), (gy + 4 - n) % 4
                wait_if(l, y, piece(l, y, (s4, r4), (j, n, k - 1), gx=gx), west)

    def to_mate(part, start):
        h = core if start else 1 - core
        rows = pl.ds(0, 2304) if part == 0 else pl.ds(256 + 768 * (part - 1), 256)
        view = W.at[h, min(part, 1), rows]
        return remote(view, view, s5.at[part], r5.at[part], gx=gx + 1 - 2 * core)

    for part in range(4):
        to_mate(part, True).start()
        sent.append(to_mate(part, True).wait_send)
    film_in.wait()
    halo_in(1)
    to_mate(0, False).wait_recv()

    row = film[ids[0]]
    mult_a, shift_a, mult_b, shift_b = 1.0 + row[0:1], row[1:2], 1.0 + row[2:3], row[3:4]

    def half(h, block, tap):
        return W[h, block, pl.ds(pl.multiple_of(tap * 256, 256), 256), :]

    def weight(block, tap):
        return jnp.concatenate([half(0, block, tap), half(1, block, tap)], axis=1)

    taps = [(0, 1, 1 + 3), (0, 0, 1), (0, 2, 7)] + [(1, a, 3 * a + 2 - 2 * west) for a in (1, 0, 2)]

    def rows_of(m):
        return pl.ds(pl.multiple_of(m * ROWS, ROWS), ROWS)

    def send_hidden(m):
        return remote(H.at[0, rows_of(m)], H.at[1, rows_of(m)], cs.at[m], cr.at[m], gy=(gy + 2) % 4)

    @pl.loop(0, CHUNKS)
    def _(m):
        r = rows_of(m)
        pre = jnp.zeros((ROWS, 256), F32)
        for col, a, tap in taps:
            pre = pre + jnp.dot(X[col, a, r, :], weight(0, tap), preferred_element_type=F32)
        pre = pre * mult_a + shift_a
        sig = sigmoid(pre)
        H[0, r, :] = (X[0, 1, r, :].astype(F32) + pre * sig).astype(BF16)
        DA[r, :] = mult_a * sig * (1.0 + pre * (1.0 - sig))
        send_hidden(m).start()

    @sent.append
    def _():
        @pl.loop(0, CHUNKS)
        def _(m):
            send_hidden(m).wait_send()

    for part in range(1, 4):
        to_mate(part, False).wait_recv()
    south = gy // 2

    def back_dot(value, tap):
        turned = (((1,), (1,)), ((), ()))
        return lax.dot_general(
            value[:, :128], half(0, 1, tap), turned, preferred_element_type=F32
        ) + lax.dot_general(value[:, 128:], half(1, 1, tap), turned, preferred_element_type=F32)

    @pl.loop(0, CHUNKS)
    def _(m):
        r = rows_of(m)
        ACC[r, :] = jnp.dot(H[0, r, :], weight(1, 4), preferred_element_type=F32)
        FAR[r, :] = jnp.dot(H[0, r, :], weight(1, 1 + 6 * south), preferred_element_type=F32)

    for a in range(3):
        XT[1, a] = X[1, a].T
    cot_out.wait_recv()

    @pl.loop(0, CHUNKS)
    def _(m):
        r = rows_of(m)
        send_hidden(m).wait_recv()
        other = H[1, r, :]
        pre = ACC[r, :] + jnp.dot(other, weight(1, 7 - 6 * south), preferred_element_type=F32)
        pre = pre * mult_b + shift_b
        sig = sigmoid(pre)
        out[r, :] = (H[0, r, :].astype(F32) + pre * sig).astype(BF16)
        up = cot[r, :].astype(F32)
        near_grad = (up * mult_b * sig * (1.0 + pre * (1.0 - sig))).astype(BF16)
        pre = jnp.dot(other, weight(1, 4), preferred_element_type=F32) + FAR[r, :]
        pre = pre * mult_b + shift_b
        sig = sigmoid(pre)
        far_grad = (cot_far[r, :].astype(F32) * mult_b * sig * (1.0 + pre * (1.0 - sig))).astype(BF16)
        back = up + back_dot(near_grad, 4) + back_dot(far_grad, 1 + 6 * south)
        value = back * DA[r, :]
        left, right = value[:, :128], value[:, 128:]
        GA[r, :] = jnp.concatenate(
            [jnp.where(core == 0, left, right), jnp.where(core == 0, right, left)], axis=1
        ).astype(BF16)

    scale = 1.0 / 512.0

    def mate(tap):
        at = pl.ds(pl.multiple_of(tap * 256, 256), 256)
        return remote(TB.at[at], RC.at[at], m1.at[tap], q1.at[tap], gx=gx + 1 - 2 * core)

    def rows72(l, y):
        return pl.ds(pl.multiple_of((l * 4 + y) * 72, 8), 72)

    def empty(l, y):
        number = 4 * l + y
        first = ((number >= 0) & (number <= 2)) | ((number >= 11) & (number <= 13)) | ((number >= 22) & (number <= 23))
        last = ((number >= 8) & (number <= 9)) | ((number >= 18) & (number <= 20)) | (number >= 29)
        return ((west == 0) & first) | ((west == 1) & last)

    def sum_y(k, l):
        return remote(T.at[k - 1, l], RY.at[k - 1, l], m2.at[k - 1, l], q2.at[k - 1, l], gy=(gy + k) % 4)

    def send_rows(a, first, last):
        for col in range(2):
            mate(row_taps[a][col][2]).wait_recv()

        @pl.loop(first, last)
        def _(l):
            for k in order:
                at = rows72(l, (gy + k) % 4)

                @pl.when(jnp.logical_not(empty(l, (gy + k) % 4)))
                def _():
                    T[k - 1, l] = (TA[at, :] + RC[at, :]).astype(BF16)
                    sum_y(k, l).start()

    row_taps = [[(0, a, 3 * a + 1), (1, a, 3 * a + 2 - 2 * west)] for a in range(3)]
    parts = ((0, 2), (2, 5), (5, 8))
    for a in range(3):
        for col, _, tap in row_taps[a]:
            at = pl.ds(pl.multiple_of(tap * 256, 256), 256)
            term = jnp.dot(XT[col, a], GA[...], preferred_element_type=F32) * scale
            TB[at, :] = term[:, 128:]
            mate(tap).start()
            sent.append(mate(tap).wait_send)
            TA[at, :] = term[:, :128]
        if a:
            send_rows(a - 1, *parts[a - 1])
    send_rows(2, *parts[2])

    @sent.append
    def _():
        for k in order:

            @pl.loop(0, 8)
            def _(l):
                @pl.when(jnp.logical_not(empty(l, (gy + k) % 4)))
                def _():
                    sum_y(k, l).wait_send()

    @pl.loop(0, 8)
    def _(l):
        at = rows72(l, gy)
        A2[l] = TA[at, :] + RC[at, :]

    def sum_x(k, h):
        part = pl.ds(4 * h, 4)
        return remote(XB.at[k - 1, part], PX.at[k - 1, part], m3.at[k - 1, h], q3.at[k - 1, h], gx=(gx + 4 * k) % 16)

    def window(xx, h):
        return A2[4 * h : 4 * h + 4, pl.ds(pl.multiple_of(xx * 16, 16), 24), :]

    for h in range(2):
        for k in order:

            @pl.loop(4 * h, 4 * h + 4)
            def _(l):
                @pl.when(jnp.logical_not(empty(l, gy)))
                def _():
                    sum_y(k, l).wait_recv()
                    A2[l] += RY[k - 1, l].astype(F32)

        for k in order:
            XB[k - 1, 4 * h : 4 * h + 4] = window((x + k) % 4, h).astype(BF16)
            sum_x(k, h).start()
            sent.append(sum_x(k, h).wait_send)

    def sum_z(k):
        z = (zid + k) % 16
        return remote(ZB.at[z // 8, z % 8], ZR.at[k], m4.at[k], q4.at[k], **ring(k))

    for h in range(2):
        P = window(x, h)
        for k in order:
            sum_x(k, h).wait_recv()
            P = P + PX[k - 1, 4 * h : 4 * h + 4].astype(F32)
        PP[4 * h : 4 * h + 4] = P
        ZB[0, 4 * h : 4 * h + 4] = P[:, 0:16].astype(BF16)
        ZB[1, 4 * h : 4 * h + 4] = P[:, 8:24].astype(BF16)
        for k in far_first:

            @pl.when((zid + k) % 8 // 4 == h)
            def _():
                sum_z(k).start()

    for k in far_first:
        sent.append(sum_z(k).wait_send)
    total = PP[lead, pl.ds(pl.multiple_of(zh * 8, 8), 16), :]
    for k in far_first[::-1]:
        sum_z(k).wait_recv()
        total = total + ZR[k].astype(F32)
    RR[core] = total
    swap = remote(RR.at[core], RR.at[core], m5, q5, gx=gx + 1 - 2 * core)
    swap_in = remote(RR.at[1 - core], RR.at[1 - core], m5, q5, gx=gx + 1 - 2 * core)
    swap.start()
    sent.append(swap.wait_send)
    swap_in.wait_recv()
    for j in range(9):
        grad[j : j + 1, :] = RR[(j + core) % 2, pl.ds(2 * x + zh + (9 * core + j) // 2, 1), :]
    finish()


def shards(inputs, lead_ids, film, flat_weights, cotangent):
    padded = jnp.pad(flat_weights.reshape(2, 9, 128), ((0, 0), (0, 7), (0, 0)))
    vmem = pl.BlockSpec(memory_space=pltpu.VMEM)
    hbm = pl.BlockSpec(memory_space=pltpu.HBM)
    outputs, total = pl.pallas_call(
        step_kernel,
        out_shape=(jax.ShapeDtypeStruct((512, 256), BF16), jax.ShapeDtypeStruct((9, 128), F32)),
        in_specs=[pl.BlockSpec(memory_space=pltpu.SMEM), vmem, hbm, hbm, hbm],
        out_specs=(vmem, vmem),
        scratch_shapes=[
            pltpu.VMEM((2, 2, 2304, 128), BF16),
            pltpu.VMEM((2, 8, 2, 16, 128), BF16),
            pltpu.VMEM((2, 4, 2, 2, 2, 16, 128), BF16),
            pltpu.VMEM((2, 3, 512, 256), BF16),
            pltpu.VMEM((2, 3, 256, 512), BF16),
            pltpu.VMEM((2, 512, 256), BF16),
            pltpu.VMEM((512, 256), BF16),
            pltpu.VMEM((512, 256), F32),
            pltpu.VMEM((512, 256), F32),
            pltpu.VMEM((512, 256), F32),
            pltpu.VMEM((2304, 128), F32),
            pltpu.VMEM((2304, 128), F32),
            pltpu.VMEM((2304, 128), F32),
            pltpu.VMEM((3, 8, 72, 128), BF16),
            pltpu.VMEM((3, 8, 72, 128), BF16),
            pltpu.VMEM((8, 72, 128), F32),
            pltpu.VMEM((3, 8, 24, 128), BF16),
            pltpu.VMEM((3, 8, 24, 128), BF16),
            pltpu.VMEM((8, 24, 128), F32),
            pltpu.VMEM((2, 8, 16, 128), BF16),
            pltpu.VMEM((16, 16, 128), BF16),
            pltpu.VMEM((2, 16, 128), F32),
            pltpu.VMEM((360, 4, 256), F32),
            pltpu.VMEM((512, 256), BF16),
            pltpu.VMEM((512, 256), BF16),
            DMA((3,)),
            DMA((4, 2)), DMA((4, 2)),
            DMA((CHUNKS,)), DMA((CHUNKS,)),
            DMA(()), DMA(()),
            DMA((16,)), DMA((16,)),
            DMA((16,)), DMA((2, 4, 2)),
            DMA((2, 3)), DMA((2, 3)),
            DMA((2, 4, 3)), DMA((2, 4, 3)),
            DMA((4,)), DMA((4,)),
            DMA((9,)), DMA((9,)),
            DMA((3, 8)), DMA((3, 8)),
            DMA((3, 2)), DMA((3, 2)),
            DMA((16,)), DMA((16,)),
            DMA(()), DMA(()),
        ],
        compiler_params=pltpu.CompilerParams(
            collective_id=0, has_side_effects=True, vmem_limit_bytes=50 << 20
        ),
    )(lead_ids, padded, inputs.reshape(512, 256), film, cotangent.reshape(512, 256))
    return (outputs.reshape(inputs.shape), total.reshape(-1))


def solution(mesh):
    return jax.shard_map(
        shards,
        mesh=mesh,
        in_specs=(
            P("lead", "gy", "gx", None),
            P("lead"),
            P(),
            P(None, ("lead", "gy", "gx")),
            P("lead", "gy", "gx", None),
        ),
        out_specs=(P("lead", "gy", "gx", None), P(("lead", "gy", "gx"))),
        check_vma=False,
    )
```
